256 devices in a mesh: sec: 4 (over y), ty: 32 (over z, x), tx: 2 (over core).
Axes of the slice: x: 4, y: 4, z: 8, core: 2. Of those that a mesh axis runs over, the one named last changes fastest.
Arguments:
- images: float32 [4, 2048, 1024], P('sec', 'ty', 'tx'), may hold values from -6 to 6
- tissue_rows: int32 [32], replicated, may hold values from 21 to 64, as said below
Outputs:
- aligned_flow: float32 [2, 4, 2048, 1024], P(None, 'sec', 'ty', 'tx')
The draws below stay inside these ranges and needn't reach their ends.
Inputs may be any that keep to these rules, and one draw needn't show every extreme that they name: `tissue_rows`: tissue row counts grow along the rows of tiles, about threefold from the first to the last.
All inputs are finite; a program needn't handle non-finite values.
Results may differ from the reference program's by a relative error of at most 0.00002.
Values sent between devices are 32-bit elements; how exact they have to be, the bound alone decides.
A program may use at most 64 MiB of HBM per device.

```python
import jax
import jax.numpy as jnp
from jax import lax

TR = 64
SWEEPS = 12
RELAX = 4
RESTRICT = 4
S = 4
H = 2048
W = 1024
N_TY = 32


def draw_tissue_rows(key, part):
    tiles = jnp.arange(N_TY, dtype=jnp.int32)
    base = TR // 3 + tiles * (TR - TR // 3) // max(N_TY - 1, 1)
    jitter = jax.random.randint(key, (N_TY,), 0, TR // 8 + 1)
    return jnp.minimum(base + jitter, TR).astype(jnp.int32)


def block_scale(stream_key, extent, pieces, low, top_value):
    factor_of = 1.0
    for position, blocks in pieces:
        steps = jax.random.uniform(jax.random.fold_in(jax.random.fold_in(stream_key, 6), position), (blocks,), jnp.float32, low / len(pieces), top_value / len(pieces))
        factor_of = factor_of * jnp.repeat(jnp.exp(steps), extent[position] // blocks).reshape((-1,) + (1,) * (len(extent) - 1 - position))
    return factor_of


def gaussian(own_key, dims, deviation, reach, shards=(), kind=jnp.bfloat16):
    level = block_scale(own_key, dims, shards, -0.22, 0.18) if shards else 1.0
    entries = jax.random.normal(own_key, dims, jnp.float32) * deviation * level
    return jnp.minimum(jnp.maximum(entries, -reach), reach).astype(kind)


def setup_inputs(seed: int = 0) -> dict:
    key_of = jax.random.split(jax.random.key(seed), 3)
    return {
        "images": gaussian(key_of[0], (S, H, W), 1.0, 6.0, ((0, 4), (1, 32), (2, 2)), jnp.float32),
        "tissue_rows": draw_tissue_rows(jax.random.fold_in(key_of[2], 71), 0),
    }


alpha_term = 0.5
stack_weight = 1.0
mesh_weight = 0.5
relax_total = 5.0


def tissue_mask(tissue_rows):
    row_ids = jnp.arange(H, dtype=jnp.int32)
    tile = row_ids // TR
    local = row_ids - tile * TR
    limit = jnp.take(tissue_rows, tile).astype(jnp.int32)
    inside = ((local + limit // 2) % TR) < limit
    return inside.astype(jnp.float32)[:, None] * jnp.ones((1, W), jnp.float32)


def pair_flow(first, second, mask):
    wide_a = jnp.pad(first, 1)
    wide_b = jnp.pad(second, 1)
    grad_x = 0.25 * ((wide_a[1:-1, 2:] - wide_a[1:-1, :-2]) + (wide_b[1:-1, 2:] - wide_b[1:-1, :-2]))
    grad_y = 0.25 * ((wide_a[2:, 1:-1] - wide_a[:-2, 1:-1]) + (wide_b[2:, 1:-1] - wide_b[:-2, 1:-1]))
    grad_t = second - first
    denom = alpha_term + grad_x * grad_x + grad_y * grad_y
    flow = jnp.zeros((2, H, W), jnp.float32)
    for sweep in range(SWEEPS):
        padded = jnp.pad(flow, ((0, 0), (1, 1), (1, 1)))
        mean = 0.25 * ((padded[:, :-2, 1:-1] + padded[:, 2:, 1:-1]) + (padded[:, 1:-1, :-2] + padded[:, 1:-1, 2:]))
        share = (grad_x * mean[0] + grad_y * mean[1] + grad_t) / denom
        flow = jnp.stack([mean[0] - grad_x * share, mean[1] - grad_y * share]) * mask
    return flow


def reference(images, tissue_rows):
    mask = tissue_mask(tissue_rows)
    following = jnp.concatenate([images[1:], images[-1:]], 0)
    flows = lax.map(lambda pair: pair_flow(pair[0], pair[1], mask), (images, following))
    flows = jnp.transpose(flows, (1, 0, 2, 3))
    coarse = flows.reshape(2, S, H // RESTRICT, RESTRICT, W // RESTRICT, RESTRICT).mean(axis=(3, 5))
    disp = coarse
    for sweep in range(RELAX):
        padded = jnp.pad(disp, ((0, 0), (1, 1), (1, 1), (1, 1)))
        stack_sum = padded[:, :-2, 1:-1, 1:-1] + padded[:, 2:, 1:-1, 1:-1]
        mesh_sum = (padded[:, 1:-1, :-2, 1:-1] + padded[:, 1:-1, 2:, 1:-1]) + (padded[:, 1:-1, 1:-1, :-2] + padded[:, 1:-1, 1:-1, 2:])
        disp = (coarse + stack_weight * stack_sum + mesh_weight * mesh_sum) / relax_total
    back = jnp.repeat(jnp.repeat(disp, RESTRICT, axis=2), RESTRICT, axis=3)
    return flows + mask * back
```

```python
import functools

import jax
import jax.numpy as jnp
import numpy as np
from jax import lax
from jax.experimental import pallas as pl
from jax.experimental.pallas import tpu as pltpu
from jax.sharding import PartitionSpec as P

MESH = pl.DeviceIdType.MESH
F32 = jnp.float32
BF16 = jnp.bfloat16

SWEEPS = 12
RELAX = 4
ALPHA = 0.5
STACK = 1.0
COUPLE = 0.5
TOTAL = 5.0

N_SEC = 4
ROWS = 64
COLS = 512
HALO = 32
EXT = ROWS + 2 * HALO
NM = EXT // 8
TILES = 5
STEP = 104


def section_table():
    w = {(0, 0): 1.0}
    for _ in range(RELAX):
        new = {(0, 0): 1.0}
        for (a, b), value in w.items():
            new[(a + 1, b)] = new.get((a + 1, b), 0.0) + value
            new[(a, b + 1)] = new.get((a, b + 1), 0.0) + value
        w = {key: value / TOTAL for key, value in new.items()}
    path = np.zeros((N_SEC, N_SEC))
    for i in range(N_SEC - 1):
        path[i, i + 1] = path[i + 1, i] = STACK
    table = np.zeros((N_SEC, N_SEC, RELAX + 1))
    for (a, b), value in w.items():
        power = np.linalg.matrix_power(path, a)
        for src in range(N_SEC):
            for shift in range(N_SEC):
                table[src, shift, b] += value * power[(src + shift) % N_SEC, src] * COUPLE**b
    return table.astype(np.float32).reshape(-1)


def split3(x):
    hi = x.astype(BF16)
    rest = x - hi.astype(F32)
    mid = rest.astype(BF16)
    low = (rest - mid.astype(F32)).astype(BF16)
    return jnp.concatenate([hi, mid, low], axis=0)


def dot3(x, w):
    n = x.shape[0]
    y = jnp.dot(split3(x), w, preferred_element_type=F32)
    return y[:n] + y[n : 2 * n] + y[2 * n :]


def kernel(
    tissue_ref, table_ref, img_ref, out_ref,
    own, nxt, coef, flow, pooled, pool_w, up_w, sent, got, packed, outbuf,
    load_sem, send_sem, recv_sem, csend_sem, crecv_sem, out_sem,
):
    n_ty = lax.axis_size("ty")
    sec = lax.axis_index("sec")
    ty = lax.axis_index("ty")
    tx = lax.axis_index("tx")
    before = {"ty": lax.rem(ty + n_ty - 1, n_ty)}
    after = {"ty": lax.rem(ty + 1, n_ty)}
    partner = {"tx": 1 - tx}
    others = [{"sec": lax.rem(sec + d, N_SEC)} for d in range(1, N_SEC)]

    loads = [
        pltpu.make_async_copy(
            img_ref.at[0, :, pl.ds(128 * j, 128)], own.at[j, pl.ds(HALO, ROWS), :], load_sem.at[j]
        )
        for j in range(4)
    ]
    for load in loads:
        load.start()

    barrier = pltpu.get_barrier_semaphore()
    peers = [before, after, partner] + others
    for peer in peers:
        pl.semaphore_signal(barrier, inc=1, device_id=peer, device_id_type=MESH)

    lane = lax.broadcasted_iota(jnp.int32, (8, 128), 1)
    sub = lax.broadcasted_iota(jnp.int32, (8, 128), 0)

    def start_of(j):
        return jnp.where(tx == 0, STEP * j - 1, 385 - STEP * j)

    n_id = lax.broadcasted_iota(jnp.int32, (128, 256), 1)
    k_id = lax.broadcasted_iota(jnp.int32, (128, 256), 0)
    q_of = jnp.where(n_id < 128, n_id - 8, n_id - 24)
    for j in range(TILES):
        col = k_id + start_of(j)
        lo, hi = (12, 115)
        if j == 0:
            lo = jnp.where(tx == 0, 1, 12)
            hi = jnp.where(tx == 0, 115, 126)
        hit = (k_id >= lo) & (k_id <= hi) & (lax.shift_right_arithmetic(col, 2) == q_of)
        pool_w[pl.ds(128 * j, 128), :] = jnp.where(hit, 0.0625, 0.0).astype(BF16)
    un = lax.broadcasted_iota(jnp.int32, (128, 128), 1)
    uq = lax.broadcasted_iota(jnp.int32, (128, 128), 0)
    for i in range(4):
        a = jnp.where(tx == 0, i, 3 - i)
        hit = lax.shift_right_arithmetic(un + 128 * a, 2) == uq
        up_w[:, pl.ds(128 * i, 128)] = jnp.where(hit, 1.0, 0.0).astype(BF16)

    for load in loads:
        load.wait()
    pl.semaphore_wait(barrier, len(peers))

    edge = jnp.where(tx == 0, 3, 0)
    top, mid, low = (pl.ds(HALO, HALO), pl.ds(HALO, ROWS), pl.ds(ROWS, HALO))
    head, tail = (pl.ds(0, HALO), pl.ds(HALO + ROWS, HALO))
    four = pl.ds(0, 4)

    def send(k, src, dst, device):
        copy = pltpu.make_async_remote_copy(
            src_ref=src, dst_ref=dst, send_sem=send_sem.at[k], recv_sem=recv_sem.at[k],
            device_id=device, device_id_type=MESH,
        )
        copy.start()
        return copy

    previous = {"sec": lax.rem(sec + N_SEC - 1, N_SEC)}
    c0 = send(0, own.at[four, top], nxt.at[four, top], previous)
    c1 = send(1, own.at[four, low], nxt.at[four, low], previous)
    c2 = send(2, own.at[four, top], own.at[four, tail], before)
    c3 = send(3, own.at[four, low], own.at[four, head], after)
    c4 = send(4, own.at[edge, mid], own.at[4, mid], partner)
    c0.wait_recv()
    c5 = send(5, nxt.at[four, top], nxt.at[four, tail], before)
    c6 = send(6, nxt.at[edge, top], nxt.at[4, top], partner)
    c1.wait_recv()
    c7 = send(7, nxt.at[four, low], nxt.at[four, head], after)
    c8 = send(8, nxt.at[edge, low], nxt.at[4, low], partner)
    c2.wait_recv()
    c9 = send(9, own.at[edge, tail], own.at[4, tail], partner)
    c3.wait_recv()
    c10 = send(10, own.at[edge, head], own.at[4, head], partner)
    c5.wait_recv()
    c11 = send(11, nxt.at[edge, tail], nxt.at[4, tail], partner)
    c7.wait_recv()
    c12 = send(12, nxt.at[edge, head], nxt.at[4, head], partner)
    copies = [c0, c1, c2, c3, c4, c5, c6, c7, c8, c9, c10, c11, c12]

    k_own = tissue_ref[ty]
    k_before = jnp.where(ty > 0, tissue_ref[lax.rem(ty + n_ty - 1, n_ty)], 0)
    k_after = jnp.where(ty < n_ty - 1, tissue_ref[lax.rem(ty + 1, n_ty)], 0)
    limit = jnp.where(sub < 2, k_before, jnp.where(sub < 6, k_own, k_after))
    row0 = NM * sub + (ROWS * ty - HALO)

    def tile_body(j, carry):
        @pl.when(j == 4)
        def _():
            for c in (c4, c6, c8, c9, c10, c11, c12):
                c.wait_recv()

        start = start_of(j)
        pos = lax.rem(start + 640, 640)
        ta = pos // 128
        tb = lax.rem(ta + 1, TILES)
        off = pos - 128 * ta
        ta = jnp.where((j == 0) & (ta == 4), 0, ta)
        tb = jnp.where((j == 0) & (tb == 4), 3, tb)
        shift = lax.rem(128 - off, 128)
        from_a = lane < 128 - off
        col = lane + (start + COLS * tx)
        col_in = (col >= 0) & (col < 2 * COLS)
        last = sec == N_SEC - 1
        s_list, d_list, m_list = ([], [], [])
        for m in range(NM):
            rows = pl.ds(m, 8, stride=NM)
            oa = own[ta, rows, :]
            ob = own[tb, rows, :]
            na = jnp.where(last, oa, nxt[ta, rows, :])
            nb = jnp.where(last, ob, nxt[tb, rows, :])
            row = row0 + m
            inside = (row >= 0) & (row < ROWS * n_ty) & col_in
            s_m = jnp.where(
                from_a, pltpu.roll(oa + na, shift, axis=1), pltpu.roll(ob + nb, shift, axis=1)
            )
            d_m = jnp.where(
                from_a, pltpu.roll(na - oa, shift, axis=1), pltpu.roll(nb - ob, shift, axis=1)
            )
            s_list.append(jnp.where(inside, s_m, 0.0))
            d_list.append(d_m)
            local = NM * sub + (m + HALO)
            tissue = ((local + lax.shift_right_logical(limit, 1)) & (ROWS - 1)) < limit
            m_list.append(jnp.where(tissue & col_in, 1.0, 0.0))
        for m in range(NM):
            up = s_list[m - 1] if m else pltpu.roll(s_list[NM - 1], 1, axis=0)
            down = s_list[m + 1] if m < NM - 1 else pltpu.roll(s_list[0], 7, axis=0)
            gx = 0.25 * (pltpu.roll(s_list[m], 127, axis=1) - pltpu.roll(s_list[m], 1, axis=1))
            gy = 0.25 * (down - up)
            gt = d_list[m]
            xx = gx * gx
            yy = gy * gy
            r = m_list[m] / (ALPHA + xx + yy)
            q = 0.25 * r
            coef[0, m] = (ALPHA + yy) * q
            coef[1, m] = gx * gy * q
            coef[2, m] = gx * gt * r
            coef[3, m] = (ALPHA + xx) * q
            coef[4, m] = gy * gt * r

        def around(x, m):
            up = x[m - 1] if m else pltpu.roll(x[NM - 1], 1, axis=0)
            down = x[m + 1] if m < NM - 1 else pltpu.roll(x[0], 7, axis=0)
            return (up + down) + (pltpu.roll(x[m], 1, axis=1) + pltpu.roll(x[m], 127, axis=1))

        def sweep(_, uv):
            u, v = (uv[:NM], uv[NM:])
            new_u, new_v = ([], [])
            for m in range(NM):
                mu = around(u, m)
                mv = around(v, m)
                b = coef[1, m]
                new_u.append(coef[0, m] * mu - b * mv - coef[2, m])
                new_v.append(coef[3, m] * mv - b * mu - coef[4, m])
            return tuple(new_u + new_v)

        first = [-coef[2, m] for m in range(NM)] + [-coef[4, m] for m in range(NM)]
        uv = lax.fori_loop(0, SWEEPS - 1, sweep, tuple(first))
        for c in range(2):
            for p in range(4):
                f = uv[16 * c + 4 * p : 16 * c + 4 * p + 4]
                pooled[pl.ds(8 * (4 * c + p), 8), pl.ds(pl.multiple_of(128 * j, 128), 128)] = (
                    f[0] + f[1]
                ) + (f[2] + f[3])
            for m in range(NM):
                flow[c, j, m] = uv[16 * c + m]
        return carry

    lax.fori_loop(0, TILES, tile_body, 0)

    coarse = dot3(pooled[...], pool_w[...])
    crow = 4 * sub + (16 * ty - 8)
    cmask = []
    for p in range(4):
        row_in = (crow + p >= 0) & (crow + p < 16 * n_ty)
        per_tile = []
        for t in range(2):
            q = lane + (128 * tx + (-8 if t == 0 else 104))
            per_tile.append(jnp.where(row_in & (q >= 0) & (q < 256), 1.0, 0.0))
        cmask.append(per_tile)
    e = [
        [[coarse[8 * (4 * c + p) : 8 * (4 * c + p) + 8, 128 * t : 128 * t + 128] for p in range(4)] for t in range(2)]
        for c in range(2)
    ]

    def mesh_sweep(x, t):
        out = []
        for p in range(4):
            up = x[p - 1] if p else pltpu.roll(x[3], 1, axis=0)
            down = x[p + 1] if p < 3 else pltpu.roll(x[0], 7, axis=0)
            total = (up + down) + (pltpu.roll(x[p], 1, axis=1) + pltpu.roll(x[p], 127, axis=1))
            out.append(total * cmask[p][t])
        return out

    def pack(e):
        out = []
        for p in range(4):
            both = [
                jnp.where(lane < 116, pltpu.roll(e[c][0][p], 120, axis=1), pltpu.roll(e[c][1][p], 104, axis=1))
                for c in range(2)
            ]
            out.append(jnp.where(sub < 4, pltpu.roll(both[0], 6, axis=0), pltpu.roll(both[1], 2, axis=0)))
        return out

    terms = [pack(e)]
    for _ in range(RELAX):
        e = [[mesh_sweep(e[c][t], t) for t in range(2)] for c in range(2)]
        terms.append(pack(e))
    base = sec * (N_SEC * (RELAX + 1))

    def combine(d):
        out = []
        for p in range(4):
            total = table_ref[base + d * (RELAX + 1)] * terms[0][p]
            for b in range(1, RELAX + 1):
                total = total + table_ref[base + d * (RELAX + 1) + b] * terms[b][p]
            out.append(total)
        return out

    shifts = (2, 1, 3)
    for d in shifts:
        for p, x in enumerate(combine(d)):
            sent[d - 1, p] = x
    mine = combine(0)
    exchanges = []
    for d in shifts:
        copy = pltpu.make_async_remote_copy(
            src_ref=sent.at[d - 1], dst_ref=got.at[d - 1],
            send_sem=csend_sem.at[d - 1], recv_sem=crecv_sem.at[d - 1],
            device_id=others[d - 1], device_id_type=MESH,
        )
        copy.start()
        exchanges.append(copy)

    for i in range(4):
        sh1 = jnp.where(tx == 0, 127 - 24 * i, 24 * i + 1)
        sh2 = jnp.where(tx == 0, 103 - 24 * i, 25 + 24 * i)
        take = jnp.where(tx == 0, lane, 127 - lane) < 115 - 24 * i

        def gather(m, carry, i=i, sh1=sh1, sh2=sh2, take=take):
            def both(j):
                return jnp.where(
                    sub < 4, pltpu.roll(flow[0, j, m], 6, axis=0), pltpu.roll(flow[1, j, m], 2, axis=0)
                )

            packed[i, m] = jnp.where(
                take, pltpu.roll(both(i), sh1, axis=1), pltpu.roll(both(i + 1), sh2, axis=1)
            )
            return carry

        lax.fori_loop(0, NM, gather, 0)

    for copy in exchanges:
        copy.wait_recv()
    disp = [((mine[p] + got[0, p]) + (got[1, p] + got[2, p])) for p in range(4)]
    back = dot3(jnp.concatenate(disp, axis=0), up_w[...])
    outs = []
    for i in range(4):
        a = jnp.where(tx == 0, i, 3 - i)
        for m in range(NM):
            p = m // 4
            local = NM * (sub & 3) + m
            tissue = ((local + lax.shift_right_logical(k_own, 1)) & (ROWS - 1)) < k_own
            value = packed[i, m] + jnp.where(tissue, back[8 * p : 8 * p + 8, 128 * i : 128 * i + 128], 0.0)
            outbuf[i, pl.ds(m, 8, stride=NM), :] = value
        for c in range(2):
            copy = pltpu.make_async_copy(
                outbuf.at[i, pl.ds(ROWS * c, ROWS), :],
                out_ref.at[c, 0, :, pl.ds(pl.multiple_of(128 * a, 128), 128)],
                out_sem.at[2 * i + c],
            )
            copy.start()
            outs.append(copy)
    for copy in copies:
        copy.wait_send()
    for copy in exchanges:
        copy.wait_send()
    for copy in outs:
        copy.wait()


def shards(images, tissue_rows, table):
    vmem = pltpu.VMEM
    return pl.pallas_call(
        kernel,
        out_shape=jax.ShapeDtypeStruct((2, 1, ROWS, COLS), F32),
        in_specs=[
            pl.BlockSpec(memory_space=pltpu.SMEM),
            pl.BlockSpec(memory_space=pltpu.SMEM),
            pl.BlockSpec(memory_space=pl.ANY),
        ],
        out_specs=pl.BlockSpec(memory_space=pl.ANY),
        scratch_shapes=[
            vmem((TILES, EXT, 128), F32),
            vmem((TILES, EXT, 128), F32),
            vmem((5, NM, 8, 128), F32),
            vmem((2, TILES, NM, 8, 128), F32),
            vmem((64, TILES * 128), F32),
            vmem((TILES * 128, 256), BF16),
            vmem((128, COLS), BF16),
            vmem((3, 4, 8, 128), F32),
            vmem((3, 4, 8, 128), F32),
            vmem((4, NM, 8, 128), F32),
            vmem((4, EXT, 128), F32),
            pltpu.SemaphoreType.DMA((4,)),
            pltpu.SemaphoreType.DMA((13,)),
            pltpu.SemaphoreType.DMA((13,)),
            pltpu.SemaphoreType.DMA((3,)),
            pltpu.SemaphoreType.DMA((3,)),
            pltpu.SemaphoreType.DMA((8,)),
        ],
        compiler_params=pltpu.CompilerParams(
            collective_id=0, has_side_effects=True, vmem_limit_bytes=16 * 1024 * 1024
        ),
        name="align",
    )(tissue_rows, table, images)


def solution(mesh):
    placed = (P("sec", "ty", "tx"), P(), P())
    mapped = jax.shard_map(
        shards, mesh=mesh, in_specs=placed, out_specs=P(None, "sec", "ty", "tx"), check_vma=False
    )

    def run(images, tissue_rows):
        return mapped(images, tissue_rows, jnp.asarray(section_table()))

    return run
```

```python
import functools

import jax
import jax.numpy as jnp
import numpy as np
from jax import lax
from jax.experimental import pallas as pl
from jax.experimental.pallas import tpu as pltpu
from jax.sharding import PartitionSpec as P

MESH = pl.DeviceIdType.MESH
F32 = jnp.float32
BF16 = jnp.bfloat16

SWEEPS = 12
RELAX = 4
ALPHA = 0.5
STACK = 1.0
COUPLE = 0.5
TOTAL = 5.0

N_SEC = 4
ROWS = 64
COLS = 512
HALO = 32
EXT = ROWS + 2 * HALO
NM = EXT // 8
TILES = 5
STEP = 104


def section_table():
    w = {(0, 0): 1.0}
    for _ in range(RELAX):
        new = {(0, 0): 1.0}
        for (a, b), value in w.items():
            new[(a + 1, b)] = new.get((a + 1, b), 0.0) + value
            new[(a, b + 1)] = new.get((a, b + 1), 0.0) + value
        w = {key: value / TOTAL for key, value in new.items()}
    path = np.zeros((N_SEC, N_SEC))
    for i in range(N_SEC - 1):
        path[i, i + 1] = path[i + 1, i] = STACK
    table = np.zeros((N_SEC, N_SEC, RELAX + 1))
    for (a, b), value in w.items():
        power = np.linalg.matrix_power(path, a)
        for src in range(N_SEC):
            for shift in range(N_SEC):
                table[src, shift, b] += value * power[(src + shift) % N_SEC, src] * COUPLE**b
    return table.astype(np.float32)


TABLE = section_table()


def split3(x):
    hi = x.astype(BF16)
    rest = x - hi.astype(F32)
    mid = rest.astype(BF16)
    low = (rest - mid.astype(F32)).astype(BF16)
    return jnp.concatenate([hi, mid, low], axis=0)


def dot3(x, w):
    n = x.shape[0]
    y = jnp.dot(split3(x), w, preferred_element_type=F32)
    return y[:n] + y[n : 2 * n] + y[2 * n :]


def kernel(
    tissue_hbm, img_ref, out_ref,
    own, nxt, coef, fa, fb, pooled, pool_w, up_w, sent, got, packed, tissue_ref,
    load_sem, send_sem, recv_sem, csend_sem, crecv_sem,
):
    n_ty = lax.axis_size("ty")
    sec = lax.axis_index("sec")
    ty = lax.axis_index("ty")
    tx = lax.axis_index("tx")
    has_before, has_after = (ty > 0, ty < n_ty - 1)
    has_next, has_prev = (sec < N_SEC - 1, sec > 0)
    ty_b, ty_a = (jnp.maximum(ty - 1, 0), jnp.minimum(ty + 1, n_ty - 1))
    sec_n, sec_p = (jnp.minimum(sec + 1, N_SEC - 1), jnp.maximum(sec - 1, 0))
    partner = {"tx": 1 - tx}
    others = [{"sec": (sec + d) & (N_SEC - 1)} for d in range(1, N_SEC)]
    top, mid, low = (pl.ds(HALO, HALO), pl.ds(HALO, ROWS), pl.ds(ROWS, HALO))
    head, tail = (pl.ds(0, HALO), pl.ds(HALO + ROWS, HALO))
    four = pl.ds(0, 4)

    loads = [
        pltpu.make_async_copy(img_ref.at[0, :, pl.ds(128 * j, 128)], own.at[j, mid], load_sem.at[j])
        for j in range(4)
    ]
    for load in loads:
        load.start()
    tissue_load = pltpu.make_async_copy(tissue_hbm, tissue_ref, load_sem.at[4])
    tissue_load.start()

    barrier = pltpu.get_barrier_semaphore()
    meets = [(None, partner)] + [(None, d) for d in others]
    meets += [(has_before, {"ty": ty_b}), (has_after, {"ty": ty_a})]
    for has_sec, s_at in ((has_next, sec_n), (has_prev, sec_p)):
        meets += [
            (has_sec & has_before, {"sec": s_at, "ty": ty_b}),
            (has_sec & has_after, {"sec": s_at, "ty": ty_a}),
        ]

    def when(cond, fn):
        if cond is None:
            fn()
        else:
            pl.when(cond)(fn)

    n_meets = 0
    for cond, device in meets:
        when(cond, lambda device=device: pl.semaphore_signal(barrier, inc=1, device_id=device, device_id_type=MESH))
        n_meets = n_meets + (1 if cond is None else cond.astype(jnp.int32))

    lane = lax.broadcasted_iota(jnp.int32, (8, 128), 1)
    sub = lax.broadcasted_iota(jnp.int32, (8, 128), 0)

    def start_of(j):
        return jnp.where(tx == 0, STEP * j - 1, 385 - STEP * j)

    def clear(rows):
        def body():
            for ref in (own, nxt):
                for j in range(TILES):
                    ref[j, rows, :] = jnp.zeros((HALO, 128), F32)
        return body

    n_id = lax.broadcasted_iota(jnp.int32, (128, 256), 1)
    k_id = lax.broadcasted_iota(jnp.int32, (128, 256), 0)
    q_of = jnp.where(n_id < 128, n_id - 8, n_id - 24)
    for j in range(TILES):
        col = k_id + start_of(j)
        lo, hi = (12, 115)
        if j == 0:
            lo = jnp.where(tx == 0, 1, 12)
            hi = jnp.where(tx == 0, 115, 126)
        hit = (k_id >= lo) & (k_id <= hi) & (lax.shift_right_arithmetic(col, 2) == q_of)
        pool_w[pl.ds(128 * j, 128), :] = jnp.where(hit, 0.0625, 0.0).astype(BF16)
    un = lax.broadcasted_iota(jnp.int32, (128, 128), 1)
    uq = lax.broadcasted_iota(jnp.int32, (128, 128), 0)
    for i in range(4):
        a = jnp.where(tx == 0, i, 3 - i)
        hit = lax.shift_right_arithmetic(un + 128 * a, 2) == uq
        up_w[:, pl.ds(128 * i, 128)] = jnp.where(hit, 1.0, 0.0).astype(BF16)
    pl.when(jnp.logical_not(has_before))(clear(head))
    pl.when(jnp.logical_not(has_after))(clear(tail))

    for load in loads:
        load.wait()
    tissue_load.wait()
    pl.semaphore_wait(barrier, n_meets)

    edge = jnp.where(tx == 0, 3, 0)

    def remote(k, src, dst, device):
        return pltpu.make_async_remote_copy(
            src_ref=src, dst_ref=dst, send_sem=send_sem.at[k], recv_sem=recv_sem.at[k],
            device_id=device, device_id_type=MESH,
        )

    up_b, dn_a = (has_before, has_after)
    corner_t = (remote(0, own.at[four, top], nxt.at[four, tail], {"sec": sec_p, "ty": ty_b}), has_prev & up_b, has_next & dn_a)
    corner_h = (remote(1, own.at[four, low], nxt.at[four, head], {"sec": sec_p, "ty": ty_a}), has_prev & dn_a, has_next & up_b)
    next_mid = (remote(2, own.at[four, mid], nxt.at[four, mid], {"sec": sec_p}), has_prev, has_next)
    own_t = (remote(3, own.at[four, top], own.at[four, tail], {"ty": ty_b}), up_b, dn_a)
    own_h = (remote(4, own.at[four, low], own.at[four, head], {"ty": ty_a}), dn_a, up_b)
    side = (remote(5, own.at[edge, mid], own.at[4, mid], partner), None, None)
    side_ot = (remote(6, own.at[edge, tail], own.at[4, tail], partner), dn_a, dn_a)
    side_oh = (remote(7, own.at[edge, head], own.at[4, head], partner), up_b, up_b)
    side_m = (remote(8, nxt.at[edge, mid], nxt.at[4, mid], partner), has_next, has_next)
    side_t = (remote(9, nxt.at[edge, tail], nxt.at[4, tail], partner), has_next & dn_a, has_next & dn_a)
    side_h = (remote(10, nxt.at[edge, head], nxt.at[4, head], partner), has_next & up_b, has_next & up_b)
    copies = [corner_t, corner_h, next_mid, own_t, own_h, side, side_ot, side_oh, side_m, side_t, side_h]

    for copy, sends, _ in copies[:6]:
        when(sends, copy.start)
    for first, second in ((own_t, side_ot), (own_h, side_oh), (corner_t, side_t), (corner_h, side_h), (next_mid, side_m)):
        when(first[2], first[0].wait_recv)
        when(second[1], second[0].start)

    k_own = tissue_ref[ty]
    k_before = jnp.where(has_before, tissue_ref[ty_b], 0)
    k_after = jnp.where(has_after, tissue_ref[ty_a], 0)
    limit = jnp.where(sub < 2, k_before, jnp.where(sub < 6, k_own, k_after))
    half = lax.shift_right_logical(limit, 1)
    row0 = NM * sub + (ROWS * ty - HALO)
    last = jnp.logical_not(has_next)

    def shifted(x, m):
        up = x[m - 1] if m else pltpu.roll(x[NM - 1], 1, axis=0)
        down = x[m + 1] if m < NM - 1 else pltpu.roll(x[0], 7, axis=0)
        return up, down

    def coefficients(j, carry):
        @pl.when(j == 4)
        def _():
            for copy, _, receives in copies[5:]:
                when(receives, copy.wait_recv)

        start = start_of(j)
        pos = jnp.where(start < 0, start + 640, start)
        ta = lax.shift_right_logical(pos, 7)
        off = pos & 127
        tb = jnp.where(ta == 4, 0, ta + 1)
        ta = jnp.where((j == 0) & (ta == 4), 0, ta)
        tb = jnp.where((j == 0) & (tb == 4), 3, tb)
        shift = (128 - off) & 127
        from_a = lane < 128 - off
        col = lane + (start + COLS * tx)
        col_in = (col >= 0) & (col < 2 * COLS)
        s_list, d_list, m_list = ([], [], [])
        for m in range(NM):
            rows = pl.ds(m, 8, stride=NM)
            oa = own[ta, rows, :]
            ob = own[tb, rows, :]
            na = jnp.where(last, oa, nxt[ta, rows, :])
            nb = jnp.where(last, ob, nxt[tb, rows, :])
            row = row0 + m
            inside = (row >= 0) & (row < ROWS * n_ty) & col_in
            s_m = jnp.where(
                from_a, pltpu.roll(oa + na, shift, axis=1), pltpu.roll(ob + nb, shift, axis=1)
            )
            d_m = jnp.where(
                from_a, pltpu.roll(na - oa, shift, axis=1), pltpu.roll(nb - ob, shift, axis=1)
            )
            s_list.append(jnp.where(inside, s_m, 0.0))
            d_list.append(d_m)
            local = NM * sub + (m + HALO)
            tissue = ((local + half) & (ROWS - 1)) < limit
            m_list.append(jnp.where(tissue & col_in, 1.0, 0.0))
        for m in range(NM):
            up, down = shifted(s_list, m)
            gx = 0.25 * (pltpu.roll(s_list[m], 127, axis=1) - pltpu.roll(s_list[m], 1, axis=1))
            gy = 0.25 * (down - up)
            gt = d_list[m]
            xx = gx * gx
            yy = gy * gy
            r = m_list[m] / (ALPHA + xx + yy)
            q = 0.25 * r
            rt = gt * r
            coef[0, j, m] = (ALPHA + yy) * q
            coef[1, j, m] = gx * gy * q
            coef[2, j, m] = -(gx * rt)
            coef[3, j, m] = (ALPHA + xx) * q
            coef[4, j, m] = -(gy * rt)
        return carry

    lax.fori_loop(0, TILES, coefficients, 0)

    def sweep(read, dst):
        for j in range(TILES):
            u = [read(0, j, m) for m in range(NM)]
            v = [read(1, j, m) for m in range(NM)]
            for m in range(NM):
                means = []
                for x in (u, v):
                    up, down = shifted(x, m)
                    means.append((up + down) + (pltpu.roll(x[m], 1, axis=1) + pltpu.roll(x[m], 127, axis=1)))
                mu, mv = means
                b = coef[1, j, m]
                dst[0, j, m] = (coef[0, j, m] * mu - b * mv) + coef[2, j, m]
                dst[1, j, m] = (coef[3, j, m] * mv - b * mu) + coef[4, j, m]

    def of(ref):
        return lambda c, j, m: ref[c, j, m]

    sweep(lambda c, j, m: coef[2 + 2 * c, j, m], fa)

    def two_sweeps(_, carry):
        sweep(of(fa), fb)
        sweep(of(fb), fa)
        return carry

    lax.fori_loop(0, (SWEEPS - 2) // 2, two_sweeps, 0)

    for c in range(2):
        for p in range(4):
            for j in range(TILES):
                f = [fa[c, j, 4 * p + k] for k in range(4)]
                pooled[pl.ds(8 * (4 * c + p), 8), pl.ds(128 * j, 128)] = (f[0] + f[1]) + (f[2] + f[3])

    coarse = dot3(pooled[...], pool_w[...])
    crow = 4 * sub + (16 * ty - 8)
    cmask = []
    for p in range(4):
        row_in = (crow + p >= 0) & (crow + p < 16 * n_ty)
        per_tile = []
        for t in range(2):
            q = lane + (128 * tx + (-8 if t == 0 else 104))
            per_tile.append(jnp.where(row_in & (q >= 0) & (q < 256), 1.0, 0.0))
        cmask.append(per_tile)
    e = [
        [[coarse[8 * (4 * c + p) : 8 * (4 * c + p) + 8, 128 * t : 128 * t + 128] for p in range(4)] for t in range(2)]
        for c in range(2)
    ]

    def mesh_sweep(x, t):
        out = []
        for p in range(4):
            up = x[p - 1] if p else pltpu.roll(x[3], 1, axis=0)
            down = x[p + 1] if p < 3 else pltpu.roll(x[0], 7, axis=0)
            total = (up + down) + (pltpu.roll(x[p], 1, axis=1) + pltpu.roll(x[p], 127, axis=1))
            out.append(total * cmask[p][t])
        return out

    def pack(e):
        out = []
        for p in range(4):
            both = [
                jnp.where(lane < 116, pltpu.roll(e[c][0][p], 120, axis=1), pltpu.roll(e[c][1][p], 104, axis=1))
                for c in range(2)
            ]
            out.append(jnp.where(sub < 4, pltpu.roll(both[0], 6, axis=0), pltpu.roll(both[1], 2, axis=0)))
        return out

    terms = [pack(e)]
    for _ in range(RELAX):
        e = [[mesh_sweep(e[c][t], t) for t in range(2)] for c in range(2)]
        terms.append(pack(e))

    def weight(d, b):
        value = TABLE[N_SEC - 1, d, b]
        for src in range(N_SEC - 1):
            value = jnp.where(sec == src, TABLE[src, d, b], value)
        return value

    def combine(d):
        w = [weight(d, b) for b in range(RELAX + 1)]
        out = []
        for p in range(4):
            total = w[0] * terms[0][p]
            for b in range(1, RELAX + 1):
                total = total + w[b] * terms[b][p]
            out.append(total)
        return out

    shifts = (2, 1, 3)
    for d in shifts:
        for p, x in enumerate(combine(d)):
            sent[d - 1, p] = x
    mine = combine(0)
    exchanges = []
    for d in shifts:
        copy = pltpu.make_async_remote_copy(
            src_ref=sent.at[d - 1], dst_ref=got.at[d - 1],
            send_sem=csend_sem.at[d - 1], recv_sem=crecv_sem.at[d - 1],
            device_id=others[d - 1], device_id_type=MESH,
        )
        copy.start()
        exchanges.append(copy)

    shift_1 = [jnp.where(tx == 0, 127 - 24 * i, 24 * i + 1) for i in range(4)]
    shift_2 = [jnp.where(tx == 0, 103 - 24 * i, 25 + 24 * i) for i in range(4)]
    from_edge = jnp.where(tx == 0, lane, 127 - lane)
    for m in range(NM):
        both = [
            jnp.where(sub < 4, pltpu.roll(fa[0, j, m], 6, axis=0), pltpu.roll(fa[1, j, m], 2, axis=0))
            for j in range(TILES)
        ]
        for i in range(4):
            packed[i, m] = jnp.where(
                from_edge < 115 - 24 * i,
                pltpu.roll(both[i], shift_1[i], axis=1), pltpu.roll(both[i + 1], shift_2[i], axis=1),
            )
    for copy, sends, _ in copies:
        when(sends, copy.wait_send)

    for copy in exchanges:
        copy.wait_recv()
    disp = [((mine[p] + got[0, p]) + (got[1, p] + got[2, p])) for p in range(4)]
    back = dot3(jnp.concatenate(disp, axis=0), up_w[...])
    for m in range(NM):
        p = m // 4
        local = NM * (sub & 3) + m
        tissue = ((local + lax.shift_right_logical(k_own, 1)) & (ROWS - 1)) < k_own
        for i in range(4):
            a = jnp.where(tx == 0, i, 3 - i)
            value = packed[i, m] + jnp.where(tissue, back[8 * p : 8 * p + 8, 128 * i : 128 * i + 128], 0.0)
            out_ref[pl.ds((m // 8) * 32 + m % 8 + 8 * a, 8, stride=64), :] = value
    for copy in exchanges:
        copy.wait_send()


def shards(images, tissue_rows):
    vmem = pltpu.VMEM
    flat = pl.pallas_call(
        kernel,
        out_shape=jax.ShapeDtypeStruct((2 * ROWS * 4, 128), F32),
        in_specs=[pl.BlockSpec(memory_space=pltpu.HBM), pl.BlockSpec(memory_space=pltpu.HBM)],
        out_specs=pl.BlockSpec(memory_space=pltpu.VMEM),
        scratch_shapes=[
            vmem((TILES, EXT, 128), F32),
            vmem((TILES, EXT, 128), F32),
            vmem((5, TILES, NM, 8, 128), F32),
            vmem((2, TILES, NM, 8, 128), F32),
            vmem((2, TILES, NM, 8, 128), F32),
            vmem((64, TILES * 128), F32),
            vmem((TILES * 128, 256), BF16),
            vmem((128, COLS), BF16),
            vmem((3, 4, 8, 128), F32),
            vmem((3, 4, 8, 128), F32),
            vmem((4, NM, 8, 128), F32),
            pltpu.SMEM((32,), jnp.int32),
            pltpu.SemaphoreType.DMA((5,)),
            pltpu.SemaphoreType.DMA((11,)),
            pltpu.SemaphoreType.DMA((11,)),
            pltpu.SemaphoreType.DMA((3,)),
            pltpu.SemaphoreType.DMA((3,)),
        ],
        compiler_params=pltpu.CompilerParams(
            collective_id=0, has_side_effects=True, vmem_limit_bytes=24 * 1024 * 1024
        ),
        name="align",
    )(tissue_rows, images)
    tiles = flat.reshape(2, ROWS // 8, 4, 8, 128).transpose(0, 1, 3, 2, 4)
    return tiles.reshape(2, 1, ROWS, COLS)


def solution(mesh):
    return jax.shard_map(
        shards, mesh=mesh, in_specs=(P("sec", "ty", "tx"), P()), out_specs=P(None, "sec", "ty", "tx"), check_vma=False
    )
```

```python
import functools

import jax
import jax.numpy as jnp
import numpy as np
from jax import lax
from jax.experimental import pallas as pl
from jax.experimental.pallas import tpu as pltpu
from jax.sharding import PartitionSpec as P

MESH = pl.DeviceIdType.MESH
F32 = jnp.float32
BF16 = jnp.bfloat16

SWEEPS = 12
RELAX = 4
ALPHA = 0.5
STACK = 1.0
COUPLE = 0.5
TOTAL = 5.0

N_SEC = 4
ROWS = 64
COLS = 512
HALO = 32
EXT = ROWS + 2 * HALO
NM = EXT // 8
TILES = 5
STEP = 104


def section_table():
    w = {(0, 0): 1.0}
    for _ in range(RELAX):
        new = {(0, 0): 1.0}
        for (a, b), value in w.items():
            new[(a + 1, b)] = new.get((a + 1, b), 0.0) + value
            new[(a, b + 1)] = new.get((a, b + 1), 0.0) + value
        w = {key: value / TOTAL for key, value in new.items()}
    path = np.zeros((N_SEC, N_SEC))
    for i in range(N_SEC - 1):
        path[i, i + 1] = path[i + 1, i] = STACK
    table = np.zeros((N_SEC, N_SEC, RELAX + 1))
    for (a, b), value in w.items():
        power = np.linalg.matrix_power(path, a)
        for src in range(N_SEC):
            for shift in range(N_SEC):
                table[src, shift, b] += value * power[(src + shift) % N_SEC, src] * COUPLE**b
    return table.astype(np.float32)


TABLE = section_table()


def split3(x):
    hi = x.astype(BF16)
    rest = x - hi.astype(F32)
    mid = rest.astype(BF16)
    low = (rest - mid.astype(F32)).astype(BF16)
    return jnp.concatenate([hi, mid, low], axis=0)


def dot3(x, w):
    n = x.shape[0]
    y = jnp.dot(split3(x), w, preferred_element_type=F32)
    return y[:n] + y[n : 2 * n] + y[2 * n :]


def kernel(
    tissue_hbm, img_ref, out_ref,
    own, nxt, sbuf, tbuf, tmask, coef, x, pooled, pool_w, up_w, sent, got, packed, tissue_ref,
    load_sem, send_sem, recv_sem, csend_sem, crecv_sem,
):
    n_ty = lax.axis_size("ty")
    sec = lax.axis_index("sec")
    ty = lax.axis_index("ty")
    tx = lax.axis_index("tx")
    has_before, has_after = (ty > 0, ty < n_ty - 1)
    has_next, has_prev = (sec < N_SEC - 1, sec > 0)
    ty_b, ty_a = (jnp.maximum(ty - 1, 0), jnp.minimum(ty + 1, n_ty - 1))
    sec_n, sec_p = (jnp.minimum(sec + 1, N_SEC - 1), jnp.maximum(sec - 1, 0))
    partner = {"tx": 1 - tx}
    others = [{"sec": (sec + d) & (N_SEC - 1)} for d in range(1, N_SEC)]
    top, mid, low = (pl.ds(HALO, HALO), pl.ds(HALO, ROWS), pl.ds(ROWS, HALO))
    head, tail = (pl.ds(0, HALO), pl.ds(HALO + ROWS, HALO))
    four = pl.ds(0, 4)

    loads = [
        pltpu.make_async_copy(img_ref.at[0, :, pl.ds(128 * j, 128)], own.at[j, mid], load_sem.at[j])
        for j in range(4)
    ]
    for load in loads:
        load.start()
    tissue_load = pltpu.make_async_copy(tissue_hbm, tissue_ref, load_sem.at[4])
    tissue_load.start()

    barrier = pltpu.get_barrier_semaphore()
    meets = [(None, partner)] + [(None, d) for d in others]
    meets += [(has_before, {"ty": ty_b}), (has_after, {"ty": ty_a})]
    for has_sec, s_at in ((has_next, sec_n), (has_prev, sec_p)):
        meets += [
            (has_sec & has_before, {"sec": s_at, "ty": ty_b}),
            (has_sec & has_after, {"sec": s_at, "ty": ty_a}),
        ]

    def when(cond, fn):
        if cond is None:
            fn()
        else:
            pl.when(cond)(fn)

    n_meets = 0
    for cond, device in meets:
        when(cond, lambda device=device: pl.semaphore_signal(barrier, inc=1, device_id=device, device_id_type=MESH))
        n_meets = n_meets + (1 if cond is None else cond.astype(jnp.int32))

    lane = lax.broadcasted_iota(jnp.int32, (8, 128), 1)
    sub = lax.broadcasted_iota(jnp.int32, (8, 128), 0)

    def start_of(j):
        return jnp.where(tx == 0, STEP * j - 1, 385 - STEP * j)

    def clear(rows):
        def body():
            for ref in (own, nxt):
                for j in range(TILES):
                    ref[j, rows, :] = jnp.zeros((HALO, 128), F32)
        return body

    n_id = lax.broadcasted_iota(jnp.int32, (128, 256), 1)
    k_id = lax.broadcasted_iota(jnp.int32, (128, 256), 0)
    q_of = jnp.where(n_id < 128, n_id - 8, n_id - 24)
    for j in range(TILES):
        col = k_id + start_of(j)
        lo, hi = (12, 115)
        if j == 0:
            lo = jnp.where(tx == 0, 1, 12)
            hi = jnp.where(tx == 0, 115, 126)
        hit = (k_id >= lo) & (k_id <= hi) & (lax.shift_right_arithmetic(col, 2) == q_of)
        pool_w[pl.ds(128 * j, 128), :] = jnp.where(hit, 0.0625, 0.0).astype(BF16)
    un = lax.broadcasted_iota(jnp.int32, (128, 128), 1)
    uq = lax.broadcasted_iota(jnp.int32, (128, 128), 0)
    for i in range(4):
        a = jnp.where(tx == 0, i, 3 - i)
        hit = lax.shift_right_arithmetic(un + 128 * a, 2) == uq
        up_w[:, pl.ds(128 * i, 128)] = jnp.where(hit, 1.0, 0.0).astype(BF16)
    pl.when(jnp.logical_not(has_before))(clear(head))
    pl.when(jnp.logical_not(has_after))(clear(tail))

    tissue_load.wait()
    k_own = tissue_ref[ty]
    k_before = jnp.where(has_before, tissue_ref[ty_b], 0)
    k_after = jnp.where(has_after, tissue_ref[ty_a], 0)
    limit = jnp.where(sub < 2, k_before, jnp.where(sub < 6, k_own, k_after))
    half = lax.shift_right_logical(limit, 1)
    for m in range(NM):
        tmask[m] = jnp.where(((NM * sub + (m + HALO) + half) & (ROWS - 1)) < limit, 1.0, 0.0)
    last = jnp.logical_not(has_next)

    for load in loads:
        load.wait()
    pl.semaphore_wait(barrier, n_meets)

    edge = jnp.where(tx == 0, 3, 0)

    def remote(k, src, dst, device):
        return pltpu.make_async_remote_copy(
            src_ref=src, dst_ref=dst, send_sem=send_sem.at[k], recv_sem=recv_sem.at[k],
            device_id=device, device_id_type=MESH,
        )

    up_b, dn_a = (has_before, has_after)
    corner_t = (remote(0, own.at[four, top], nxt.at[four, tail], {"sec": sec_p, "ty": ty_b}), has_prev & up_b, has_next & dn_a)
    corner_h = (remote(1, own.at[four, low], nxt.at[four, head], {"sec": sec_p, "ty": ty_a}), has_prev & dn_a, has_next & up_b)
    next_mid = (remote(2, own.at[four, mid], nxt.at[four, mid], {"sec": sec_p}), has_prev, has_next)
    own_t = (remote(3, own.at[four, top], own.at[four, tail], {"ty": ty_b}), up_b, dn_a)
    own_h = (remote(4, own.at[four, low], own.at[four, head], {"ty": ty_a}), dn_a, up_b)
    side = (remote(5, own.at[edge, mid], own.at[4, mid], partner), None, None)
    side_ot = (remote(6, own.at[edge, tail], own.at[4, tail], partner), dn_a, dn_a)
    side_oh = (remote(7, own.at[edge, head], own.at[4, head], partner), up_b, up_b)
    side_m = (remote(8, nxt.at[edge, mid], nxt.at[4, mid], partner), has_next, has_next)
    side_t = (remote(9, nxt.at[edge, tail], nxt.at[4, tail], partner), has_next & dn_a, has_next & dn_a)
    side_h = (remote(10, nxt.at[edge, head], nxt.at[4, head], partner), has_next & up_b, has_next & up_b)
    copies = [corner_t, corner_h, next_mid, own_t, own_h, side, side_ot, side_oh, side_m, side_t, side_h]

    for copy, sends, _ in copies[:6]:
        when(sends, copy.start)
    for first, second in ((own_t, side_ot), (own_h, side_oh), (corner_t, side_t), (corner_h, side_h), (next_mid, side_m)):
        when(first[2], first[0].wait_recv)
        when(second[1], second[0].start)

    def build(tiles):
        for side_of in range(2):
            @pl.when(tx == side_of)
            def _(side_of=side_of):
                for j in tiles:
                    start = STEP * j - 1 if side_of == 0 else 385 - STEP * j
                    ta, off = ((start + 640) % 640 // 128, start % 128)
                    tb = (ta + 1) % TILES
                    if j == 0:
                        ta, tb = (0, 0) if side_of == 0 else (3, 3)
                    for m in range(NM):
                        rows = pl.ds(m, 8, stride=NM)
                        oa = own[ta, rows, :]
                        ob = own[tb, rows, :]
                        na = jnp.where(last, oa, nxt[ta, rows, :])
                        nb = jnp.where(last, ob, nxt[tb, rows, :])
                        shift = (m - off) % 128
                        cc = (lane - m) & 127
                        from_a = cc < 128 - off
                        s_m, t_m = (
                            jnp.where(from_a, pltpu.roll(ya, shift, axis=1), pltpu.roll(yb, shift, axis=1))
                            for ya, yb in ((oa + na, ob + nb), (oa - na, ob - nb))
                        )
                        s_m = 0.25 * s_m
                        if j == 0:
                            s_m = jnp.where(cc >= 1 if side_of == 0 else cc < 127, s_m, 0.0)
                        sbuf[j, m] = s_m
                        tbuf[j, m] = t_m

    lo, hi = (jnp.where(tx == 0, 1, 0), jnp.where(tx == 0, 128, 127))

    def coefficients(j):
        s_list = [sbuf[j, m] for m in range(NM)]
        left = [pltpu.roll(v, 1, axis=1) for v in s_list]
        right = [pltpu.roll(v, 127, axis=1) for v in s_list]
        above = pltpu.roll(pltpu.roll(s_list[NM - 1], 1, axis=0), 113, axis=1)
        below = pltpu.roll(pltpu.roll(s_list[0], 7, axis=0), 15, axis=1)
        for m in range(NM):
            gx = right[m] - left[m]
            gy = (right[m + 1] if m < NM - 1 else below) - (left[m - 1] if m else above)
            mask = tmask[m]
            if j == 0:
                cc = (lane - m) & 127
                mask = jnp.where((cc >= lo) & (cc < hi), mask, 0.0)
            xx = gx * gx
            yy = ALPHA + gy * gy
            r = mask / (xx + yy)
            q = 0.25 * r
            rt = tbuf[j, m] * r
            values = (yy * q, gx * gy * q, gx * rt, (ALPHA + xx) * q, gy * rt)
            for k, value in enumerate(values):
                if k not in (2, 4):
                    coef[0, k, j, m] = value
                    coef[1, k, j, m] = pltpu.roll(value, 1, axis=1)
                else:
                    moved = pltpu.roll(value, 1, axis=1)
                    coef[0, k, j, m] = value
                    coef[1, k, j, m] = moved
                    x[k // 2 - 1, j, m] = moved

    build(range(4))
    for j in range(4):
        coefficients(j)
    for copy, _, receives in copies[5:]:
        when(receives, copy.wait_recv)
    build((4,))
    coefficients(4)

    def sweep(kind):
        for j in range(TILES):
            means = []
            for c in range(2):
                f = [x[c, j, m] for m in range(NM)]
                below = pltpu.roll(f[0], 7, axis=0)
                above = pltpu.roll(f[NM - 1], 1, axis=0)
                g = [f[m] + f[m + 1] for m in range(NM - 1)]
                if kind == 0:
                    one = [pltpu.roll(y, 126, axis=1) for y in g]
                    one.append(pltpu.roll(f[NM - 1], 126, axis=1) + pltpu.roll(below, 14, axis=1))
                    two = [pltpu.roll(above, 112, axis=1) + f[0]] + g
                else:
                    one = g + [f[NM - 1] + pltpu.roll(below, 16, axis=1)]
                    two = [pltpu.roll(above, 114, axis=1) + pltpu.roll(f[0], 2, axis=1)]
                    two += [pltpu.roll(y, 2, axis=1) for y in g]
                means.append([one[m] + two[m] for m in range(NM)])
            for m in range(NM):
                mu, mv = (means[0][m], means[1][m])
                k = [coef[kind, i, j, m] for i in range(5)]
                x[0, j, m] = (k[0] * mu - k[1] * mv) + k[2]
                x[1, j, m] = (k[3] * mv - k[1] * mu) + k[4]

    def two_sweeps(_, carry):
        sweep(1)
        sweep(0)
        return carry

    sweep(0)
    lax.fori_loop(0, (SWEEPS - 2) // 2, two_sweeps, 0)

    for j in range(TILES):
        for c in range(2):
            for p in range(4):
                f = [pltpu.roll(x[c, j, m], (128 - m) & 127, axis=1) if m else x[c, j, m] for m in range(4 * p, 4 * p + 4)]
                pooled[pl.ds(8 * (4 * c + p), 8), pl.ds(128 * j, 128)] = (f[0] + f[1]) + (f[2] + f[3])

    coarse = dot3(pooled[...], pool_w[...])
    crow = 4 * sub + (16 * ty - 8)
    cmask = []
    for p in range(4):
        row_in = (crow + p >= 0) & (crow + p < 16 * n_ty)
        per_tile = []
        for t in range(2):
            q = lane + (128 * tx + (-8 if t == 0 else 104))
            per_tile.append(jnp.where(row_in & (q >= 0) & (q < 256), 1.0, 0.0))
        cmask.append(per_tile)
    e = [
        [[coarse[8 * (4 * c + p) : 8 * (4 * c + p) + 8, 128 * t : 128 * t + 128] for p in range(4)] for t in range(2)]
        for c in range(2)
    ]

    def mesh_sweep(y, t):
        out = []
        for p in range(4):
            up = y[p - 1] if p else pltpu.roll(y[3], 1, axis=0)
            down = y[p + 1] if p < 3 else pltpu.roll(y[0], 7, axis=0)
            total = (up + down) + (pltpu.roll(y[p], 1, axis=1) + pltpu.roll(y[p], 127, axis=1))
            out.append(total * cmask[p][t])
        return out

    def pack(e):
        out = []
        for p in range(4):
            both = [
                jnp.where(lane < 116, pltpu.roll(e[c][0][p], 120, axis=1), pltpu.roll(e[c][1][p], 104, axis=1))
                for c in range(2)
            ]
            out.append(jnp.where(sub < 4, pltpu.roll(both[0], 6, axis=0), pltpu.roll(both[1], 2, axis=0)))
        return out

    terms = [pack(e)]
    for _ in range(RELAX):
        e = [[mesh_sweep(e[c][t], t) for t in range(2)] for c in range(2)]
        terms.append(pack(e))

    def weight(d, b):
        value = TABLE[N_SEC - 1, d, b]
        for src in range(N_SEC - 1):
            value = jnp.where(sec == src, TABLE[src, d, b], value)
        return value

    def combine(d):
        w = [weight(d, b) for b in range(RELAX + 1)]
        out = []
        for p in range(4):
            total = w[0] * terms[0][p]
            for b in range(1, RELAX + 1):
                total = total + w[b] * terms[b][p]
            out.append(total)
        return out

    shifts = (2, 1, 3)
    for d in shifts:
        for p, term in enumerate(combine(d)):
            sent[d - 1, p] = term
    mine = combine(0)
    exchanges = []
    for d in shifts:
        copy = pltpu.make_async_remote_copy(
            src_ref=sent.at[d - 1], dst_ref=got.at[d - 1],
            send_sem=csend_sem.at[d - 1], recv_sem=crecv_sem.at[d - 1],
            device_id=others[d - 1], device_id_type=MESH,
        )
        copy.start()
        exchanges.append(copy)

    for side_of in range(2):
        @pl.when(tx == side_of)
        def _(side_of=side_of):
            for m in range(NM):
                both = [
                    jnp.where(sub < 4, pltpu.roll(x[0, j, m], 6, axis=0), pltpu.roll(x[1, j, m], 2, axis=0))
                    for j in range(TILES)
                ]
                for i in range(4):
                    sh1, sh2 = (127 - 24 * i, 103 - 24 * i) if side_of == 0 else (24 * i + 1, 25 + 24 * i)
                    from_edge = lane if side_of == 0 else 127 - lane
                    packed[i, m] = jnp.where(
                        from_edge < 115 - 24 * i,
                        pltpu.roll(both[i], (sh1 - m) % 128, axis=1), pltpu.roll(both[i + 1], (sh2 - m) % 128, axis=1),
                    )

    for copy, sends, _ in copies:
        when(sends, copy.wait_send)

    for copy in exchanges:
        copy.wait_recv()
    disp = [((mine[p] + got[0, p]) + (got[1, p] + got[2, p])) for p in range(4)]
    back = dot3(jnp.concatenate(disp, axis=0), up_w[...])
    for m in range(NM):
        p = m // 4
        local = NM * (sub & 3) + m
        tissue = ((local + lax.shift_right_logical(k_own, 1)) & (ROWS - 1)) < k_own
        for i in range(4):
            a = jnp.where(tx == 0, i, 3 - i)
            value = packed[i, m] + jnp.where(tissue, back[8 * p : 8 * p + 8, 128 * i : 128 * i + 128], 0.0)
            out_ref[pl.ds((m // 8) * 32 + m % 8 + 8 * a, 8, stride=64), :] = value
    for copy in exchanges:
        copy.wait_send()


def shards(images, tissue_rows):
    vmem = pltpu.VMEM
    flat = pl.pallas_call(
        kernel,
        out_shape=jax.ShapeDtypeStruct((2 * ROWS * 4, 128), F32),
        in_specs=[pl.BlockSpec(memory_space=pltpu.HBM), pl.BlockSpec(memory_space=pltpu.HBM)],
        out_specs=pl.BlockSpec(memory_space=pltpu.VMEM),
        scratch_shapes=[
            vmem((TILES, EXT, 128), F32),
            vmem((TILES, EXT, 128), F32),
            vmem((TILES, NM, 8, 128), F32),
            vmem((TILES, NM, 8, 128), F32),
            vmem((NM, 8, 128), F32),
            vmem((2, 5, TILES, NM, 8, 128), F32),
            vmem((2, TILES, NM, 8, 128), F32),
            vmem((64, TILES * 128), F32),
            vmem((TILES * 128, 256), BF16),
            vmem((128, COLS), BF16),
            vmem((3, 4, 8, 128), F32),
            vmem((3, 4, 8, 128), F32),
            vmem((4, NM, 8, 128), F32),
            pltpu.SMEM((32,), jnp.int32),
            pltpu.SemaphoreType.DMA((5,)),
            pltpu.SemaphoreType.DMA((11,)),
            pltpu.SemaphoreType.DMA((11,)),
            pltpu.SemaphoreType.DMA((3,)),
            pltpu.SemaphoreType.DMA((3,)),
        ],
        compiler_params=pltpu.CompilerParams(
            collective_id=0, has_side_effects=True, vmem_limit_bytes=24 * 1024 * 1024
        ),
        name="align",
    )(*(pltpu.with_memory_space_constraint(y, pltpu.HBM) for y in (tissue_rows, images)))
    tiles = flat.reshape(2, ROWS // 8, 4, 8, 128).transpose(0, 1, 3, 2, 4)
    return tiles.reshape(2, 1, ROWS, COLS)


def solution(mesh):
    return jax.shard_map(
        shards, mesh=mesh, in_specs=(P("sec", "ty", "tx"), P()), out_specs=P(None, "sec", "ty", "tx"), check_vma=False
    )
```

```python
import functools

import jax
import jax.numpy as jnp
import numpy as np
from jax import lax
from jax.experimental import pallas as pl
from jax.experimental.pallas import tpu as pltpu
from jax.sharding import PartitionSpec as P

MESH = pl.DeviceIdType.MESH
F32 = jnp.float32
BF16 = jnp.bfloat16

SWEEPS = 12
RELAX = 4
ALPHA = 0.5
STACK = 1.0
COUPLE = 0.5
TOTAL = 5.0

N_SEC = 4
ROWS = 64
COLS = 512
HALO = 32
EXT = ROWS + 2 * HALO
NM = EXT // 8
TILES = 5
STEP = 104


def section_table():
    w = {(0, 0): 1.0}
    for _ in range(RELAX):
        new = {(0, 0): 1.0}
        for (a, b), value in w.items():
            new[(a + 1, b)] = new.get((a + 1, b), 0.0) + value
            new[(a, b + 1)] = new.get((a, b + 1), 0.0) + value
        w = {key: value / TOTAL for key, value in new.items()}
    path = np.zeros((N_SEC, N_SEC))
    for i in range(N_SEC - 1):
        path[i, i + 1] = path[i + 1, i] = STACK
    table = np.zeros((N_SEC, N_SEC, RELAX + 1))
    for (a, b), value in w.items():
        power = np.linalg.matrix_power(path, a)
        for src in range(N_SEC):
            for shift in range(N_SEC):
                table[src, shift, b] += value * power[(src + shift) % N_SEC, src] * COUPLE**b
    return table.astype(np.float32)


TABLE = section_table()


def split3(x):
    hi = x.astype(BF16)
    rest = x - hi.astype(F32)
    mid = rest.astype(BF16)
    low = (rest - mid.astype(F32)).astype(BF16)
    return jnp.concatenate([hi, mid, low], axis=0)


def dot3(x, w):
    n = x.shape[0]
    y = jnp.dot(split3(x), w, preferred_element_type=F32)
    return y[:n] + y[n : 2 * n] + y[2 * n :]


def kernel(
    tissue_hbm, img_ref, out_ref,
    own, nxt, sbuf, tbuf, tmask, coef, x, pooled, pool_w, up_w, sent, got, packed, tissue_ref,
    load_sem, send_sem, recv_sem, csend_sem, crecv_sem,
):
    n_ty = lax.axis_size("ty")
    sec = lax.axis_index("sec")
    ty = lax.axis_index("ty")
    tx = lax.axis_index("tx")
    has_before, has_after = (ty > 0, ty < n_ty - 1)
    has_next, has_prev = (sec < N_SEC - 1, sec > 0)
    ty_b, ty_a = (jnp.maximum(ty - 1, 0), jnp.minimum(ty + 1, n_ty - 1))
    sec_n, sec_p = (jnp.minimum(sec + 1, N_SEC - 1), jnp.maximum(sec - 1, 0))
    partner = {"tx": 1 - tx}
    others = [{"sec": (sec + d) & (N_SEC - 1)} for d in range(1, N_SEC)]
    top, mid, low = (pl.ds(HALO, HALO), pl.ds(HALO, ROWS), pl.ds(ROWS, HALO))
    head, tail = (pl.ds(0, HALO), pl.ds(HALO + ROWS, HALO))
    four = pl.ds(0, 4)

    loads = [
        pltpu.make_async_copy(img_ref.at[0, :, pl.ds(128 * j, 128)], own.at[j, mid], load_sem.at[j])
        for j in range(4)
    ]
    for load in loads:
        load.start()
    tissue_load = pltpu.make_async_copy(tissue_hbm, tissue_ref, load_sem.at[4])
    tissue_load.start()

    barrier = pltpu.get_barrier_semaphore()
    meets = [(None, partner)] + [(None, d) for d in others]
    meets += [(has_before, {"ty": ty_b}), (has_after, {"ty": ty_a})]
    for has_sec, s_at in ((has_next, sec_n), (has_prev, sec_p)):
        meets += [
            (has_sec & has_before, {"sec": s_at, "ty": ty_b}),
            (has_sec & has_after, {"sec": s_at, "ty": ty_a}),
        ]

    def when(cond, fn):
        if cond is None:
            fn()
        else:
            pl.when(cond)(fn)

    n_meets = 0
    for cond, device in meets:
        when(cond, lambda device=device: pl.semaphore_signal(barrier, inc=1, device_id=device, device_id_type=MESH))
        n_meets = n_meets + (1 if cond is None else cond.astype(jnp.int32))

    lane = lax.broadcasted_iota(jnp.int32, (8, 128), 1)
    sub = lax.broadcasted_iota(jnp.int32, (8, 128), 0)

    def start_of(j):
        return jnp.where(tx == 0, STEP * j - 1, 385 - STEP * j)

    def clear(rows):
        def body():
            for ref in (own, nxt):
                for j in range(TILES):
                    ref[j, rows, :] = jnp.zeros((HALO, 128), F32)
        return body

    n_id = lax.broadcasted_iota(jnp.int32, (128, 256), 1)
    k_id = lax.broadcasted_iota(jnp.int32, (128, 256), 0)
    q_of = jnp.where(n_id < 128, n_id - 8, n_id - 24)
    for j in range(TILES):
        col = k_id + start_of(j)
        lo, hi = (12, 115)
        if j == 0:
            lo = jnp.where(tx == 0, 1, 12)
            hi = jnp.where(tx == 0, 115, 126)
        hit = (k_id >= lo) & (k_id <= hi) & (lax.shift_right_arithmetic(col, 2) == q_of)
        pool_w[pl.ds(128 * j, 128), :] = jnp.where(hit, 0.0625, 0.0).astype(BF16)
    un = lax.broadcasted_iota(jnp.int32, (128, 128), 1)
    uq = lax.broadcasted_iota(jnp.int32, (128, 128), 0)
    for i in range(4):
        a = jnp.where(tx == 0, i, 3 - i)
        hit = lax.shift_right_arithmetic(un + 128 * a, 2) == uq
        up_w[:, pl.ds(128 * i, 128)] = jnp.where(hit, 1.0, 0.0).astype(BF16)
    pl.when(jnp.logical_not(has_before))(clear(head))
    pl.when(jnp.logical_not(has_after))(clear(tail))

    tissue_load.wait()
    k_own = tissue_ref[ty]
    k_before = jnp.where(has_before, tissue_ref[ty_b], 0)
    k_after = jnp.where(has_after, tissue_ref[ty_a], 0)
    limit = jnp.where(sub < 2, k_before, jnp.where(sub < 6, k_own, k_after))
    half = lax.shift_right_logical(limit, 1)
    for m in range(NM):
        tmask[m] = jnp.where(((NM * sub + (m + HALO) + half) & (ROWS - 1)) < limit, 1.0, 0.0)
    last = jnp.logical_not(has_next)

    for load in loads:
        load.wait()
    pl.semaphore_wait(barrier, n_meets)

    edge = jnp.where(tx == 0, 3, 0)

    def remote(k, src, dst, device):
        return pltpu.make_async_remote_copy(
            src_ref=src, dst_ref=dst, send_sem=send_sem.at[k], recv_sem=recv_sem.at[k],
            device_id=device, device_id_type=MESH,
        )

    up_b, dn_a = (has_before, has_after)
    corner_t = (remote(0, own.at[four, top], nxt.at[four, tail], {"sec": sec_p, "ty": ty_b}), has_prev & up_b, has_next & dn_a)
    corner_h = (remote(1, own.at[four, low], nxt.at[four, head], {"sec": sec_p, "ty": ty_a}), has_prev & dn_a, has_next & up_b)
    next_mid = (remote(2, own.at[four, mid], nxt.at[four, mid], {"sec": sec_p}), has_prev, has_next)
    own_t = (remote(3, own.at[four, top], own.at[four, tail], {"ty": ty_b}), up_b, dn_a)
    own_h = (remote(4, own.at[four, low], own.at[four, head], {"ty": ty_a}), dn_a, up_b)
    side = (remote(5, own.at[edge, mid], own.at[4, mid], partner), None, None)
    side_ot = (remote(6, own.at[edge, tail], own.at[4, tail], partner), dn_a, dn_a)
    side_oh = (remote(7, own.at[edge, head], own.at[4, head], partner), up_b, up_b)
    side_m = (remote(8, nxt.at[edge, mid], nxt.at[4, mid], partner), has_next, has_next)
    side_t = (remote(9, nxt.at[edge, tail], nxt.at[4, tail], partner), has_next & dn_a, has_next & dn_a)
    side_h = (remote(10, nxt.at[edge, head], nxt.at[4, head], partner), has_next & up_b, has_next & up_b)
    copies = [corner_t, corner_h, next_mid, own_t, own_h, side, side_ot, side_oh, side_m, side_t, side_h]

    for copy, sends, _ in copies[:6]:
        when(sends, copy.start)
    for first, second in ((own_t, side_ot), (own_h, side_oh), (corner_t, side_t), (corner_h, side_h), (next_mid, side_m)):
        when(first[2], first[0].wait_recv)
        when(second[1], second[0].start)

    def build(tiles):
        for side_of in range(2):
            @pl.when(tx == side_of)
            def _(side_of=side_of):
                for j in tiles:
                    start = STEP * j - 1 if side_of == 0 else 385 - STEP * j
                    ta, off = ((start + 640) % 640 // 128, start % 128)
                    tb = (ta + 1) % TILES
                    if j == 0:
                        ta, tb = (0, 0) if side_of == 0 else (3, 3)
                    for m in range(NM):
                        rows = pl.ds(m, 8, stride=NM)
                        oa = own[ta, rows, :]
                        ob = own[tb, rows, :]
                        na = jnp.where(last, oa, nxt[ta, rows, :])
                        nb = jnp.where(last, ob, nxt[tb, rows, :])
                        shift = (m - off) % 128
                        cc = (lane - m) & 127
                        from_a = cc < 128 - off
                        s_m, t_m = (
                            jnp.where(from_a, pltpu.roll(ya, shift, axis=1), pltpu.roll(yb, shift, axis=1))
                            for ya, yb in ((oa + na, ob + nb), (oa - na, ob - nb))
                        )
                        s_m = 0.25 * s_m
                        if j == 0:
                            s_m = jnp.where(cc >= 1 if side_of == 0 else cc < 127, s_m, 0.0)
                        sbuf[j, m] = s_m
                        tbuf[j, m] = t_m

    lo, hi = (jnp.where(tx == 0, 1, 0), jnp.where(tx == 0, 128, 127))

    def coefficients(j):
        s_list = [sbuf[j, m] for m in range(NM)]
        for frame in range(2):
            left = [pltpu.roll(v, 1 + frame, axis=1) for v in s_list]
            right = s_list if frame else [pltpu.roll(v, 127, axis=1) for v in s_list]
            above = pltpu.roll(pltpu.roll(s_list[NM - 1], 1, axis=0), 113 + frame, axis=1)
            below = pltpu.roll(pltpu.roll(s_list[0], 7, axis=0), 15 + frame, axis=1)
            for m in range(NM):
                gx = right[m] - left[m]
                gy = (right[m + 1] if m < NM - 1 else below) - (left[m - 1] if m else above)
                gt = pltpu.roll(tbuf[j, m], 1, axis=1) if frame else tbuf[j, m]
                mask = tmask[m]
                if j == 0:
                    cc = (lane - (m + frame)) & 127
                    mask = jnp.where((cc >= lo) & (cc < hi), mask, 0.0)
                xx = gx * gx
                yy = ALPHA + gy * gy
                r = mask / (xx + yy)
                q = 0.25 * r
                rt = gt * r
                values = (yy * q, gx * gy * q, gx * rt, (ALPHA + xx) * q, gy * rt)
                for k, value in enumerate(values):
                    coef[frame, k, j, m] = value
                if frame:
                    x[0, j, m] = values[2]
                    x[1, j, m] = values[4]

    build(range(4))
    for j in range(4):
        coefficients(j)
    for copy, _, receives in copies[5:]:
        when(receives, copy.wait_recv)
    build((4,))
    coefficients(4)

    def sweep(kind):
        for j in range(TILES):
            means = []
            for c in range(2):
                f = [x[c, j, m] for m in range(NM)]
                below = pltpu.roll(f[0], 7, axis=0)
                above = pltpu.roll(f[NM - 1], 1, axis=0)
                g = [f[m] + f[m + 1] for m in range(NM - 1)]
                if kind == 0:
                    one = [pltpu.roll(y, 126, axis=1) for y in g]
                    one.append(pltpu.roll(f[NM - 1], 126, axis=1) + pltpu.roll(below, 14, axis=1))
                    two = [pltpu.roll(above, 112, axis=1) + f[0]] + g
                else:
                    one = g + [f[NM - 1] + pltpu.roll(below, 16, axis=1)]
                    two = [pltpu.roll(above, 114, axis=1) + pltpu.roll(f[0], 2, axis=1)]
                    two += [pltpu.roll(y, 2, axis=1) for y in g]
                means.append([one[m] + two[m] for m in range(NM)])
            for m in range(NM):
                mu, mv = (means[0][m], means[1][m])
                k = [coef[kind, i, j, m] for i in range(5)]
                x[0, j, m] = (k[0] * mu - k[1] * mv) + k[2]
                x[1, j, m] = (k[3] * mv - k[1] * mu) + k[4]

    def two_sweeps(_, carry):
        sweep(1)
        sweep(0)
        return carry

    sweep(0)
    lax.fori_loop(0, (SWEEPS - 2) // 2, two_sweeps, 0)

    for j in range(TILES):
        for c in range(2):
            for p in range(4):
                f = [pltpu.roll(x[c, j, m], (128 - m) & 127, axis=1) if m else x[c, j, m] for m in range(4 * p, 4 * p + 4)]
                pooled[pl.ds(8 * (4 * c + p), 8), pl.ds(128 * j, 128)] = (f[0] + f[1]) + (f[2] + f[3])

    coarse = dot3(pooled[...], pool_w[...])
    crow = 4 * sub + (16 * ty - 8)
    cmask = []
    for p in range(4):
        row_in = (crow + p >= 0) & (crow + p < 16 * n_ty)
        per_tile = []
        for t in range(2):
            q = lane + (128 * tx + (-8 if t == 0 else 104))
            per_tile.append(jnp.where(row_in & (q >= 0) & (q < 256), 1.0, 0.0))
        cmask.append(per_tile)
    e = [
        [[coarse[8 * (4 * c + p) : 8 * (4 * c + p) + 8, 128 * t : 128 * t + 128] for p in range(4)] for t in range(2)]
        for c in range(2)
    ]

    def mesh_sweep(y, t):
        out = []
        for p in range(4):
            up = y[p - 1] if p else pltpu.roll(y[3], 1, axis=0)
            down = y[p + 1] if p < 3 else pltpu.roll(y[0], 7, axis=0)
            total = (up + down) + (pltpu.roll(y[p], 1, axis=1) + pltpu.roll(y[p], 127, axis=1))
            out.append(total * cmask[p][t])
        return out

    def pack(e):
        out = []
        for p in range(4):
            both = [
                jnp.where(lane < 116, pltpu.roll(e[c][0][p], 120, axis=1), pltpu.roll(e[c][1][p], 104, axis=1))
                for c in range(2)
            ]
            out.append(jnp.where(sub < 4, pltpu.roll(both[0], 6, axis=0), pltpu.roll(both[1], 2, axis=0)))
        return out

    terms = [pack(e)]
    for _ in range(RELAX):
        e = [[mesh_sweep(e[c][t], t) for t in range(2)] for c in range(2)]
        terms.append(pack(e))

    def weight(d, b):
        value = TABLE[N_SEC - 1, d, b]
        for src in range(N_SEC - 1):
            value = jnp.where(sec == src, TABLE[src, d, b], value)
        return value

    def combine(d):
        w = [weight(d, b) for b in range(RELAX + 1)]
        out = []
        for p in range(4):
            total = w[0] * terms[0][p]
            for b in range(1, RELAX + 1):
                total = total + w[b] * terms[b][p]
            out.append(total)
        return out

    shifts = (2, 1, 3)
    for d in shifts:
        for p, term in enumerate(combine(d)):
            sent[d - 1, p] = term
    mine = combine(0)
    exchanges = []
    for d in shifts:
        copy = pltpu.make_async_remote_copy(
            src_ref=sent.at[d - 1], dst_ref=got.at[d - 1],
            send_sem=csend_sem.at[d - 1], recv_sem=crecv_sem.at[d - 1],
            device_id=others[d - 1], device_id_type=MESH,
        )
        copy.start()
        exchanges.append(copy)

    for side_of in range(2):
        @pl.when(tx == side_of)
        def _(side_of=side_of):
            for m in range(NM):
                both = [
                    jnp.where(sub < 4, pltpu.roll(x[0, j, m], 6, axis=0), pltpu.roll(x[1, j, m], 2, axis=0))
                    for j in range(TILES)
                ]
                for i in range(4):
                    sh1, sh2 = (127 - 24 * i, 103 - 24 * i) if side_of == 0 else (24 * i + 1, 25 + 24 * i)
                    from_edge = lane if side_of == 0 else 127 - lane
                    packed[i, m] = jnp.where(
                        from_edge < 115 - 24 * i,
                        pltpu.roll(both[i], (sh1 - m) % 128, axis=1), pltpu.roll(both[i + 1], (sh2 - m) % 128, axis=1),
                    )

    for copy, sends, _ in copies:
        when(sends, copy.wait_send)

    for copy in exchanges:
        copy.wait_recv()
    disp = [((mine[p] + got[0, p]) + (got[1, p] + got[2, p])) for p in range(4)]
    back = dot3(jnp.concatenate(disp, axis=0), up_w[...])
    for m in range(NM):
        p = m // 4
        local = NM * (sub & 3) + m
        tissue = ((local + lax.shift_right_logical(k_own, 1)) & (ROWS - 1)) < k_own
        for i in range(4):
            a = jnp.where(tx == 0, i, 3 - i)
            value = packed[i, m] + jnp.where(tissue, back[8 * p : 8 * p + 8, 128 * i : 128 * i + 128], 0.0)
            out_ref[pl.ds((m // 8) * 32 + m % 8 + 8 * a, 8, stride=64), :] = value
    for copy in exchanges:
        copy.wait_send()


def shards(images, tissue_rows):
    vmem = pltpu.VMEM
    flat = pl.pallas_call(
        kernel,
        out_shape=jax.ShapeDtypeStruct((2 * ROWS * 4, 128), F32),
        in_specs=[pl.BlockSpec(memory_space=pltpu.HBM), pl.BlockSpec(memory_space=pltpu.HBM)],
        out_specs=pl.BlockSpec(memory_space=pltpu.VMEM),
        scratch_shapes=[
            vmem((TILES, EXT, 128), F32),
            vmem((TILES, EXT, 128), F32),
            vmem((TILES, NM, 8, 128), F32),
            vmem((TILES, NM, 8, 128), F32),
            vmem((NM, 8, 128), F32),
            vmem((2, 5, TILES, NM, 8, 128), F32),
            vmem((2, TILES, NM, 8, 128), F32),
            vmem((64, TILES * 128), F32),
            vmem((TILES * 128, 256), BF16),
            vmem((128, COLS), BF16),
            vmem((3, 4, 8, 128), F32),
            vmem((3, 4, 8, 128), F32),
            vmem((4, NM, 8, 128), F32),
            pltpu.SMEM((32,), jnp.int32),
            pltpu.SemaphoreType.DMA((5,)),
            pltpu.SemaphoreType.DMA((11,)),
            pltpu.SemaphoreType.DMA((11,)),
            pltpu.SemaphoreType.DMA((3,)),
            pltpu.SemaphoreType.DMA((3,)),
        ],
        compiler_params=pltpu.CompilerParams(
            collective_id=0, has_side_effects=True, vmem_limit_bytes=24 * 1024 * 1024
        ),
        name="align",
    )(*(pltpu.with_memory_space_constraint(y, pltpu.HBM) for y in (tissue_rows, images)))
    tiles = flat.reshape(2, ROWS // 8, 4, 8, 128).transpose(0, 1, 3, 2, 4)
    return tiles.reshape(2, 1, ROWS, COLS)


def solution(mesh):
    return jax.shard_map(
        shards, mesh=mesh, in_specs=(P("sec", "ty", "tx"), P()), out_specs=P(None, "sec", "ty", "tx"), check_vma=False
    )
```

```python
import functools

import jax
import jax.numpy as jnp
import numpy as np
from jax import lax
from jax.experimental import pallas as pl
from jax.experimental.pallas import tpu as pltpu
from jax.sharding import PartitionSpec as P

MESH = pl.DeviceIdType.MESH
F32 = jnp.float32
BF16 = jnp.bfloat16

SWEEPS = 12
RELAX = 4
ALPHA = 0.5
STACK = 1.0
COUPLE = 0.5
TOTAL = 5.0

N_SEC = 4
ROWS = 64
COLS = 512
HALO = 32
REACH = 29
EXT = ROWS + 2 * HALO
NM = EXT // 8
TILES = 5
STEP = 104


def section_table():
    w = {(0, 0): 1.0}
    for _ in range(RELAX):
        new = {(0, 0): 1.0}
        for (a, b), value in w.items():
            new[(a + 1, b)] = new.get((a + 1, b), 0.0) + value
            new[(a, b + 1)] = new.get((a, b + 1), 0.0) + value
        w = {key: value / TOTAL for key, value in new.items()}
    path = np.zeros((N_SEC, N_SEC))
    for i in range(N_SEC - 1):
        path[i, i + 1] = path[i + 1, i] = STACK
    table = np.zeros((N_SEC, N_SEC, RELAX + 1))
    for (a, b), value in w.items():
        power = np.linalg.matrix_power(path, a)
        for src in range(N_SEC):
            for shift in range(N_SEC):
                table[src, shift, b] += value * power[(src + shift) % N_SEC, src] * COUPLE**b
    return table.astype(np.float32)


TABLE = section_table()


def split3(x):
    hi = x.astype(BF16)
    rest = x - hi.astype(F32)
    mid = rest.astype(BF16)
    low = (rest - mid.astype(F32)).astype(BF16)
    return jnp.concatenate([hi, mid, low], axis=0)


def dot3(x, w):
    n = x.shape[0]
    y = jnp.dot(split3(x), w, preferred_element_type=F32)
    return y[:n] + y[n : 2 * n] + y[2 * n :]


def kernel(
    tissue_hbm, img_ref, out_ref,
    own, nxt, sbuf, tbuf, tmask, coef, x, pooled, pool_w, up_w, sent, got, packed, tissue_ref,
    load_sem, send_sem, recv_sem, csend_sem, crecv_sem,
):
    n_ty = lax.axis_size("ty")
    sec = lax.axis_index("sec")
    ty = lax.axis_index("ty")
    tx = lax.axis_index("tx")
    has_before, has_after = (ty > 0, ty < n_ty - 1)
    has_next, has_prev = (sec < N_SEC - 1, sec > 0)
    ty_b, ty_a = (jnp.maximum(ty - 1, 0), jnp.minimum(ty + 1, n_ty - 1))
    sec_n, sec_p = (jnp.minimum(sec + 1, N_SEC - 1), jnp.maximum(sec - 1, 0))
    partner = {"tx": 1 - tx}
    others = [{"sec": (sec + d) & (N_SEC - 1)} for d in range(1, N_SEC)]
    top, mid, low = (pl.ds(HALO, HALO), pl.ds(HALO, ROWS), pl.ds(ROWS, HALO))
    head, tail = (pl.ds(0, HALO), pl.ds(HALO + ROWS, HALO))
    four = pl.ds(0, 4)

    for ref in (own, nxt):
        for j in range(4):
            for at in (0, EXT - 8):
                ref[j, pl.ds(at, 8), :] = jnp.zeros((8, 128), F32)

    barrier = pltpu.get_barrier_semaphore()
    meets = []
    for has_sec, s_at in ((has_next, sec_n), (has_prev, sec_p)):
        meets += [
            (has_sec & has_before, {"sec": s_at, "ty": ty_b}),
            (has_sec & has_after, {"sec": s_at, "ty": ty_a}),
        ]
    meets += [(has_before, {"ty": ty_b}), (has_after, {"ty": ty_a})]
    meets += [(None, others[d]) for d in (1, 0, 2)] + [(None, partner)]

    def when(cond, fn):
        if cond is None:
            fn()
        else:
            pl.when(cond)(fn)

    n_meets = 0
    for cond, device in meets:
        when(cond, lambda device=device: pl.semaphore_signal(barrier, inc=1, device_id=device, device_id_type=MESH))
        n_meets = n_meets + (1 if cond is None else cond.astype(jnp.int32))

    loads = [
        pltpu.make_async_copy(img_ref.at[0, :, pl.ds(128 * j, 128)], own.at[j, mid], load_sem.at[j])
        for j in range(4)
    ]
    for load in loads:
        load.start()
    tissue_load = pltpu.make_async_copy(tissue_hbm, tissue_ref, load_sem.at[4])
    tissue_load.start()

    lane = lax.broadcasted_iota(jnp.int32, (8, 128), 1)
    sub = lax.broadcasted_iota(jnp.int32, (8, 128), 0)

    def start_of(j):
        return jnp.where(tx == 0, STEP * j - 1, 385 - STEP * j)

    def clear(rows):
        def body():
            for ref in (own, nxt):
                for j in range(TILES):
                    ref[j, rows, :] = jnp.zeros((HALO, 128), F32)
        return body

    n_id = lax.broadcasted_iota(jnp.int32, (128, 256), 1)
    k_id = lax.broadcasted_iota(jnp.int32, (128, 256), 0)
    q_of = jnp.where(n_id < 128, n_id - 8, n_id - 24)
    for j in range(TILES):
        col = k_id + start_of(j)
        lo, hi = (12, 115)
        if j == 0:
            lo = jnp.where(tx == 0, 1, 12)
            hi = jnp.where(tx == 0, 115, 126)
        hit = (k_id >= lo) & (k_id <= hi) & (lax.shift_right_arithmetic(col, 2) == q_of)
        pool_w[pl.ds(128 * j, 128), :] = jnp.where(hit, 0.0625, 0.0).astype(BF16)
    un = lax.broadcasted_iota(jnp.int32, (128, 128), 1)
    uq = lax.broadcasted_iota(jnp.int32, (128, 128), 0)
    for i in range(4):
        a = jnp.where(tx == 0, i, 3 - i)
        hit = lax.shift_right_arithmetic(un + 128 * a, 2) == uq
        up_w[:, pl.ds(128 * i, 128)] = jnp.where(hit, 1.0, 0.0).astype(BF16)
    pl.when(jnp.logical_not(has_before))(clear(head))
    pl.when(jnp.logical_not(has_after))(clear(tail))

    tissue_load.wait()
    k_own = tissue_ref[ty]
    k_before = jnp.where(has_before, tissue_ref[ty_b], 0)
    k_after = jnp.where(has_after, tissue_ref[ty_a], 0)
    limit = jnp.where(sub < 2, k_before, jnp.where(sub < 6, k_own, k_after))
    half = lax.shift_right_logical(limit, 1)
    for m in range(NM):
        tmask[m] = jnp.where(((NM * sub + (m + HALO) + half) & (ROWS - 1)) < limit, 1.0, 0.0)
    last = jnp.logical_not(has_next)

    for load in loads:
        load.wait()
    pl.semaphore_wait(barrier, n_meets)

    edge = jnp.where(tx == 0, 3, 0)

    def remote(k, src, dst, device):
        return pltpu.make_async_remote_copy(
            src_ref=src, dst_ref=dst, send_sem=send_sem.at[k], recv_sem=recv_sem.at[k],
            device_id=device, device_id_type=MESH,
        )

    up_b, dn_a = (has_before, has_after)
    corner_t = (remote(0, own.at[four, pl.ds(HALO, REACH)], nxt.at[four, pl.ds(HALO + ROWS, REACH)], {"sec": sec_p, "ty": ty_b}), has_prev & up_b, has_next & dn_a)
    corner_h = (remote(1, own.at[four, pl.ds(HALO + ROWS - REACH, REACH)], nxt.at[four, pl.ds(HALO - REACH, REACH)], {"sec": sec_p, "ty": ty_a}), has_prev & dn_a, has_next & up_b)
    next_mid = (remote(2, own.at[four, mid], nxt.at[four, mid], {"sec": sec_p}), has_prev, has_next)
    own_t = (remote(3, own.at[four, pl.ds(HALO, REACH)], own.at[four, pl.ds(HALO + ROWS, REACH)], {"ty": ty_b}), up_b, dn_a)
    own_h = (remote(4, own.at[four, pl.ds(HALO + ROWS - REACH, REACH)], own.at[four, pl.ds(HALO - REACH, REACH)], {"ty": ty_a}), dn_a, up_b)
    side = (remote(5, own.at[edge, mid], own.at[4, mid], partner), None, None)
    side_ot = (remote(6, own.at[edge, tail], own.at[4, tail], partner), dn_a, dn_a)
    side_oh = (remote(7, own.at[edge, head], own.at[4, head], partner), up_b, up_b)
    side_m = (remote(8, nxt.at[edge, mid], nxt.at[4, mid], partner), has_next, has_next)
    side_t = (remote(9, nxt.at[edge, tail], nxt.at[4, tail], partner), has_next & dn_a, has_next & dn_a)
    side_h = (remote(10, nxt.at[edge, head], nxt.at[4, head], partner), has_next & up_b, has_next & up_b)
    copies = [corner_t, corner_h, next_mid, own_t, own_h, side, side_ot, side_oh, side_m, side_t, side_h]

    for copy, sends, _ in copies[:6]:
        when(sends, copy.start)
    for first, second in ((own_t, side_ot), (own_h, side_oh), (corner_t, side_t), (corner_h, side_h), (next_mid, side_m)):
        when(first[2], first[0].wait_recv)
        when(second[1], second[0].start)

    def build(tiles):
        for side_of in range(2):
            @pl.when(tx == side_of)
            def _(side_of=side_of):
                for j in tiles:
                    start = STEP * j - 1 if side_of == 0 else 385 - STEP * j
                    ta, off = ((start + 640) % 640 // 128, start % 128)
                    tb = (ta + 1) % TILES
                    if j == 0:
                        ta, tb = (0, 0) if side_of == 0 else (3, 3)
                    for m in range(NM):
                        rows = pl.ds(m, 8, stride=NM)
                        oa = own[ta, rows, :]
                        ob = own[tb, rows, :]
                        na = jnp.where(last, oa, nxt[ta, rows, :])
                        nb = jnp.where(last, ob, nxt[tb, rows, :])
                        shift = (m - off) % 128
                        cc = (lane - m) & 127
                        from_a = cc < 128 - off
                        s_m, t_m = (
                            jnp.where(from_a, pltpu.roll(ya, shift, axis=1), pltpu.roll(yb, shift, axis=1))
                            for ya, yb in ((oa + na, ob + nb), (oa - na, ob - nb))
                        )
                        s_m = 0.25 * s_m
                        if j == 0:
                            s_m = jnp.where(cc >= 1 if side_of == 0 else cc < 127, s_m, 0.0)
                        sbuf[j, m] = s_m
                        tbuf[j, m] = t_m

    lo, hi = (jnp.where(tx == 0, 1, 0), jnp.where(tx == 0, 128, 127))

    def coefficients(j):
        s_list = [sbuf[j, m] for m in range(NM)]
        for frame in range(2):
            left = [pltpu.roll(v, 1 + frame, axis=1) for v in s_list]
            right = s_list if frame else [pltpu.roll(v, 127, axis=1) for v in s_list]
            above = pltpu.roll(pltpu.roll(s_list[NM - 1], 1, axis=0), 113 + frame, axis=1)
            below = pltpu.roll(pltpu.roll(s_list[0], 7, axis=0), 15 + frame, axis=1)
            for m in range(NM):
                gx = right[m] - left[m]
                gy = (right[m + 1] if m < NM - 1 else below) - (left[m - 1] if m else above)
                gt = pltpu.roll(tbuf[j, m], 1, axis=1) if frame else tbuf[j, m]
                mask = tmask[m]
                if j == 0:
                    cc = (lane - (m + frame)) & 127
                    mask = jnp.where((cc >= lo) & (cc < hi), mask, 0.0)
                xx = gx * gx
                yy = ALPHA + gy * gy
                r = mask / (xx + yy)
                q = 0.25 * r
                rt = gt * r
                values = (yy * q, gx * gy * q, gx * rt, (ALPHA + xx) * q, gy * rt)
                for k, value in enumerate(values):
                    coef[frame, k, j, m] = value
                if frame:
                    x[0, j, m] = values[2]
                    x[1, j, m] = values[4]

    build(range(4))
    for j in range(4):
        coefficients(j)
    for copy, _, receives in copies[5:]:
        when(receives, copy.wait_recv)
    build((4,))
    coefficients(4)

    def sweep(kind):
        for j in range(TILES):
            means = []
            for c in range(2):
                f = [x[c, j, m] for m in range(NM)]
                below = pltpu.roll(f[0], 7, axis=0)
                above = pltpu.roll(f[NM - 1], 1, axis=0)
                g = [f[m] + f[m + 1] for m in range(NM - 1)]
                if kind == 0:
                    one = [pltpu.roll(y, 126, axis=1) for y in g]
                    one.append(pltpu.roll(f[NM - 1], 126, axis=1) + pltpu.roll(below, 14, axis=1))
                    two = [pltpu.roll(above, 112, axis=1) + f[0]] + g
                else:
                    one = g + [f[NM - 1] + pltpu.roll(below, 16, axis=1)]
                    two = [pltpu.roll(above, 114, axis=1) + pltpu.roll(f[0], 2, axis=1)]
                    two += [pltpu.roll(y, 2, axis=1) for y in g]
                means.append([one[m] + two[m] for m in range(NM)])
            for m in range(NM):
                mu, mv = (means[0][m], means[1][m])
                k = [coef[kind, i, j, m] for i in range(5)]
                x[0, j, m] = (k[0] * mu - k[1] * mv) + k[2]
                x[1, j, m] = (k[3] * mv - k[1] * mu) + k[4]

    def two_sweeps(_, carry):
        sweep(1)
        sweep(0)
        return carry

    sweep(0)
    for _ in range((SWEEPS - 2) // 2):
        two_sweeps(0, 0)

    for j in range(TILES):
        for c in range(2):
            for p in range(4):
                f = [pltpu.roll(x[c, j, m], (128 - m) & 127, axis=1) if m else x[c, j, m] for m in range(4 * p, 4 * p + 4)]
                pooled[pl.ds(8 * (4 * c + p), 8), pl.ds(128 * j, 128)] = (f[0] + f[1]) + (f[2] + f[3])

    coarse = dot3(pooled[...], pool_w[...])
    crow = 4 * sub + (16 * ty - 8)
    cmask = []
    for p in range(4):
        row_in = (crow + p >= 0) & (crow + p < 16 * n_ty)
        per_tile = []
        for t in range(2):
            q = lane + (128 * tx + (-8 if t == 0 else 104))
            per_tile.append(jnp.where(row_in & (q >= 0) & (q < 256), 1.0, 0.0))
        cmask.append(per_tile)
    e = [
        [[coarse[8 * (4 * c + p) : 8 * (4 * c + p) + 8, 128 * t : 128 * t + 128] for p in range(4)] for t in range(2)]
        for c in range(2)
    ]

    def mesh_sweep(y, t):
        out = []
        for p in range(4):
            up = y[p - 1] if p else pltpu.roll(y[3], 1, axis=0)
            down = y[p + 1] if p < 3 else pltpu.roll(y[0], 7, axis=0)
            total = (up + down) + (pltpu.roll(y[p], 1, axis=1) + pltpu.roll(y[p], 127, axis=1))
            out.append(total * cmask[p][t])
        return out

    def pack(e):
        out = []
        for p in range(4):
            both = [
                jnp.where(lane < 116, pltpu.roll(e[c][0][p], 120, axis=1), pltpu.roll(e[c][1][p], 104, axis=1))
                for c in range(2)
            ]
            out.append(jnp.where(sub < 4, pltpu.roll(both[0], 6, axis=0), pltpu.roll(both[1], 2, axis=0)))
        return out

    terms = [e]

    def weight(d, b):
        value = TABLE[N_SEC - 1, d, b]
        for src in range(N_SEC - 1):
            value = jnp.where(sec == src, TABLE[src, d, b], value)
        return value

    def combine(d):
        total = None
        for b in range(RELAX + 1):
            if not TABLE[:, d, b].any():
                continue
            w = weight(d, b)
            part = [[[w * y for y in terms[b][c][t]] for t in range(2)] for c in range(2)]
            total = part if total is None else [
                [[y + z for y, z in zip(total[c][t], part[c][t])] for t in range(2)] for c in range(2)
            ]
        return pack(total)

    exchanges = []
    for d in (2, 1, 3):
        while any(TABLE[:, d, b].any() for b in range(len(terms), RELAX + 1)):
            e = [[mesh_sweep(e[c][t], t) for t in range(2)] for c in range(2)]
            terms.append(e)
        for p, term in enumerate(combine(d)):
            sent[d - 1, p] = term
        copy = pltpu.make_async_remote_copy(
            src_ref=sent.at[d - 1], dst_ref=got.at[d - 1],
            send_sem=csend_sem.at[d - 1], recv_sem=crecv_sem.at[d - 1],
            device_id=others[d - 1], device_id_type=MESH,
        )
        copy.start()
        exchanges.append(copy)
    while len(terms) <= RELAX:
        e = [[mesh_sweep(e[c][t], t) for t in range(2)] for c in range(2)]
        terms.append(e)
    mine = combine(0)

    for side_of in range(2):
        @pl.when(tx == side_of)
        def _(side_of=side_of):
            for m in range(NM):
                both = [
                    jnp.where(sub < 4, pltpu.roll(x[0, j, m], 6, axis=0), pltpu.roll(x[1, j, m], 2, axis=0))
                    for j in range(TILES)
                ]
                for i in range(4):
                    sh1, sh2 = (127 - 24 * i, 103 - 24 * i) if side_of == 0 else (24 * i + 1, 25 + 24 * i)
                    from_edge = lane if side_of == 0 else 127 - lane
                    packed[i, m] = jnp.where(
                        from_edge < 115 - 24 * i,
                        pltpu.roll(both[i], (sh1 - m) % 128, axis=1), pltpu.roll(both[i + 1], (sh2 - m) % 128, axis=1),
                    )

    for copy, sends, _ in copies:
        when(sends, copy.wait_send)

    for copy in exchanges:
        copy.wait_recv()
    disp = [((mine[p] + got[0, p]) + (got[1, p] + got[2, p])) for p in range(4)]
    back = dot3(jnp.concatenate(disp, axis=0), up_w[...])
    for m in range(NM):
        p = m // 4
        local = NM * (sub & 3) + m
        tissue = ((local + lax.shift_right_logical(k_own, 1)) & (ROWS - 1)) < k_own
        for i in range(4):
            a = jnp.where(tx == 0, i, 3 - i)
            value = packed[i, m] + jnp.where(tissue, back[8 * p : 8 * p + 8, 128 * i : 128 * i + 128], 0.0)
            out_ref[pl.ds((m // 8) * 32 + m % 8 + 8 * a, 8, stride=64), :] = value
    for copy in exchanges:
        copy.wait_send()


def shards(images, tissue_rows):
    vmem = pltpu.VMEM
    flat = pl.pallas_call(
        kernel,
        out_shape=jax.ShapeDtypeStruct((2 * ROWS * 4, 128), F32),
        in_specs=[pl.BlockSpec(memory_space=pltpu.HBM), pl.BlockSpec(memory_space=pltpu.HBM)],
        out_specs=pl.BlockSpec(memory_space=pltpu.VMEM),
        scratch_shapes=[
            vmem((TILES, EXT, 128), F32),
            vmem((TILES, EXT, 128), F32),
            vmem((TILES, NM, 8, 128), F32),
            vmem((TILES, NM, 8, 128), F32),
            vmem((NM, 8, 128), F32),
            vmem((2, 5, TILES, NM, 8, 128), F32),
            vmem((2, TILES, NM, 8, 128), F32),
            vmem((64, TILES * 128), F32),
            vmem((TILES * 128, 256), BF16),
            vmem((128, COLS), BF16),
            vmem((3, 4, 8, 128), F32),
            vmem((3, 4, 8, 128), F32),
            vmem((4, NM, 8, 128), F32),
            pltpu.SMEM((32,), jnp.int32),
            pltpu.SemaphoreType.DMA((5,)),
            pltpu.SemaphoreType.DMA((11,)),
            pltpu.SemaphoreType.DMA((11,)),
            pltpu.SemaphoreType.DMA((3,)),
            pltpu.SemaphoreType.DMA((3,)),
        ],
        compiler_params=pltpu.CompilerParams(
            collective_id=0, has_side_effects=True, vmem_limit_bytes=24 * 1024 * 1024
        ),
        name="align",
    )(*(pltpu.with_memory_space_constraint(y, pltpu.HBM) for y in (tissue_rows, images)))
    tiles = flat.reshape(2, ROWS // 8, 4, 8, 128).transpose(0, 1, 3, 2, 4)
    return tiles.reshape(2, 1, ROWS, COLS)


def solution(mesh):
    return jax.shard_map(
        shards, mesh=mesh, in_specs=(P("sec", "ty", "tx"), P()), out_specs=P(None, "sec", "ty", "tx"), check_vma=False
    )
```

```python
import functools

import jax
import jax.numpy as jnp
import numpy as np
from jax import lax
from jax.experimental import pallas as pl
from jax.experimental.pallas import tpu as pltpu
from jax.sharding import PartitionSpec as P

MESH = pl.DeviceIdType.MESH
F32 = jnp.float32
BF16 = jnp.bfloat16

SWEEPS = 12
RELAX = 4
ALPHA = 0.5
STACK = 1.0
COUPLE = 0.5
TOTAL = 5.0

N_SEC = 4
ROWS = 64
COLS = 512
HALO = 32
REACH = 29
EXT = ROWS + 2 * HALO
NM = EXT // 8
TILES = 5
STEP = 104


def section_table():
    w = {(0, 0): 1.0}
    for _ in range(RELAX):
        new = {(0, 0): 1.0}
        for (a, b), value in w.items():
            new[(a + 1, b)] = new.get((a + 1, b), 0.0) + value
            new[(a, b + 1)] = new.get((a, b + 1), 0.0) + value
        w = {key: value / TOTAL for key, value in new.items()}
    path = np.zeros((N_SEC, N_SEC))
    for i in range(N_SEC - 1):
        path[i, i + 1] = path[i + 1, i] = STACK
    table = np.zeros((N_SEC, N_SEC, RELAX + 1))
    for (a, b), value in w.items():
        power = np.linalg.matrix_power(path, a)
        for src in range(N_SEC):
            for shift in range(N_SEC):
                table[src, shift, b] += value * power[(src + shift) % N_SEC, src] * COUPLE**b
    return table.astype(np.float32)


TABLE = section_table()


def split3(x):
    hi = x.astype(BF16)
    rest = x - hi.astype(F32)
    mid = rest.astype(BF16)
    low = (rest - mid.astype(F32)).astype(BF16)
    return jnp.concatenate([hi, mid, low], axis=0)


def dot3(x, w):
    n = x.shape[0]
    y = jnp.dot(split3(x), w, preferred_element_type=F32)
    return y[:n] + y[n : 2 * n] + y[2 * n :]


def kernel(
    tissue_hbm, img_ref, out_ref,
    own, nxt, sbuf, tbuf, tmask, coef, x, pooled, pool_w, up_w, sent, got, packed, tissue_ref,
    load_sem, send_sem, recv_sem, csend_sem, crecv_sem,
):
    n_ty = lax.axis_size("ty")
    sec = lax.axis_index("sec")
    ty = lax.axis_index("ty")
    tx = lax.axis_index("tx")
    has_before, has_after = (ty > 0, ty < n_ty - 1)
    has_next, has_prev = (sec < N_SEC - 1, sec > 0)
    ty_b, ty_a = (jnp.maximum(ty - 1, 0), jnp.minimum(ty + 1, n_ty - 1))
    sec_n, sec_p = (jnp.minimum(sec + 1, N_SEC - 1), jnp.maximum(sec - 1, 0))
    partner = {"tx": 1 - tx}
    others = [{"sec": (sec + d) & (N_SEC - 1)} for d in range(1, N_SEC)]
    top, mid, low = (pl.ds(HALO, HALO), pl.ds(HALO, ROWS), pl.ds(ROWS, HALO))
    head, tail = (pl.ds(0, HALO), pl.ds(HALO + ROWS, HALO))
    four = pl.ds(0, 4)

    for ref in (own, nxt):
        for j in range(4):
            for at in (0, EXT - 8):
                ref[j, pl.ds(at, 8), :] = jnp.zeros((8, 128), F32)

    barrier = pltpu.get_barrier_semaphore()
    meets = []
    for has_sec, s_at in ((has_next, sec_n), (has_prev, sec_p)):
        meets += [
            (has_sec & has_before, {"sec": s_at, "ty": ty_b}),
            (has_sec & has_after, {"sec": s_at, "ty": ty_a}),
        ]
    meets += [(has_before, {"ty": ty_b}), (has_after, {"ty": ty_a})]
    meets += [(None, others[d]) for d in (1, 0, 2)] + [(None, partner)]

    def when(cond, fn):
        if cond is None:
            fn()
        else:
            pl.when(cond)(fn)

    n_meets = 0
    for cond, device in meets:
        when(cond, lambda device=device: pl.semaphore_signal(barrier, inc=1, device_id=device, device_id_type=MESH))
        n_meets = n_meets + (1 if cond is None else cond.astype(jnp.int32))

    loads = [
        pltpu.make_async_copy(img_ref.at[0, :, pl.ds(128 * j, 128)], own.at[j, mid], load_sem.at[j])
        for j in range(4)
    ]
    for load in loads:
        load.start()
    tissue_load = pltpu.make_async_copy(tissue_hbm, tissue_ref, load_sem.at[4])
    tissue_load.start()

    lane = lax.broadcasted_iota(jnp.int32, (8, 128), 1)
    sub = lax.broadcasted_iota(jnp.int32, (8, 128), 0)

    def start_of(j):
        return jnp.where(tx == 0, STEP * j - 1, 385 - STEP * j)

    def clear(rows):
        def body():
            for ref in (own, nxt):
                for j in range(TILES):
                    ref[j, rows, :] = jnp.zeros((HALO, 128), F32)
        return body

    n_id = lax.broadcasted_iota(jnp.int32, (128, 256), 1)
    k_id = lax.broadcasted_iota(jnp.int32, (128, 256), 0)
    q_of = jnp.where(n_id < 128, n_id - 8, n_id - 24)
    for j in range(TILES):
        col = k_id + start_of(j)
        lo, hi = (12, 115)
        if j == 0:
            lo = jnp.where(tx == 0, 1, 12)
            hi = jnp.where(tx == 0, 115, 126)
        hit = (k_id >= lo) & (k_id <= hi) & (lax.shift_right_arithmetic(col, 2) == q_of)
        pool_w[pl.ds(128 * j, 128), :] = jnp.where(hit, 0.0625, 0.0).astype(BF16)
    un = lax.broadcasted_iota(jnp.int32, (128, 128), 1)
    uq = lax.broadcasted_iota(jnp.int32, (128, 128), 0)
    for i in range(4):
        a = jnp.where(tx == 0, i, 3 - i)
        hit = lax.shift_right_arithmetic(un + 128 * a, 2) == uq
        up_w[:, pl.ds(128 * i, 128)] = jnp.where(hit, 1.0, 0.0).astype(BF16)
    pl.when(jnp.logical_not(has_before))(clear(head))
    pl.when(jnp.logical_not(has_after))(clear(tail))

    tissue_load.wait()
    k_own = tissue_ref[ty]
    k_before = jnp.where(has_before, tissue_ref[ty_b], 0)
    k_after = jnp.where(has_after, tissue_ref[ty_a], 0)
    limit = jnp.where(sub < 2, k_before, jnp.where(sub < 6, k_own, k_after))
    half = lax.shift_right_logical(limit, 1)
    for m in range(NM):
        tmask[m] = jnp.where(((NM * sub + (m + HALO) + half) & (ROWS - 1)) < limit, 1.0, 0.0)
    last = jnp.logical_not(has_next)

    for load in loads:
        load.wait()
    pl.semaphore_wait(barrier, n_meets)

    edge = jnp.where(tx == 0, 3, 0)

    def remote(k, src, dst, device):
        return pltpu.make_async_remote_copy(
            src_ref=src, dst_ref=dst, send_sem=send_sem.at[k], recv_sem=recv_sem.at[k],
            device_id=device, device_id_type=MESH,
        )

    up_b, dn_a = (has_before, has_after)
    corner_t = (remote(0, own.at[four, pl.ds(HALO, REACH)], nxt.at[four, pl.ds(HALO + ROWS, REACH)], {"sec": sec_p, "ty": ty_b}), has_prev & up_b, has_next & dn_a)
    corner_h = (remote(1, own.at[four, pl.ds(HALO + ROWS - REACH, REACH)], nxt.at[four, pl.ds(HALO - REACH, REACH)], {"sec": sec_p, "ty": ty_a}), has_prev & dn_a, has_next & up_b)
    next_mid = (remote(2, own.at[four, mid], nxt.at[four, mid], {"sec": sec_p}), has_prev, has_next)
    own_t = (remote(3, own.at[four, pl.ds(HALO, REACH)], own.at[four, pl.ds(HALO + ROWS, REACH)], {"ty": ty_b}), up_b, dn_a)
    own_h = (remote(4, own.at[four, pl.ds(HALO + ROWS - REACH, REACH)], own.at[four, pl.ds(HALO - REACH, REACH)], {"ty": ty_a}), dn_a, up_b)
    side = (remote(5, own.at[edge, mid], own.at[4, mid], partner), None, None)
    side_ot = (remote(6, own.at[edge, tail], own.at[4, tail], partner), dn_a, dn_a)
    side_oh = (remote(7, own.at[edge, head], own.at[4, head], partner), up_b, up_b)
    side_m = (remote(8, nxt.at[edge, mid], nxt.at[4, mid], partner), has_next, has_next)
    side_t = (remote(9, nxt.at[edge, tail], nxt.at[4, tail], partner), has_next & dn_a, has_next & dn_a)
    side_h = (remote(10, nxt.at[edge, head], nxt.at[4, head], partner), has_next & up_b, has_next & up_b)
    copies = [corner_t, corner_h, next_mid, own_t, own_h, side, side_ot, side_oh, side_m, side_t, side_h]

    for copy, sends, _ in copies[:6]:
        when(sends, copy.start)
    def build(tiles, ref):
        for side_of in range(2):
            @pl.when(tx == side_of)
            def _(side_of=side_of):
                for j in tiles:
                    start = STEP * j - 1 if side_of == 0 else 385 - STEP * j
                    ta, off = ((start + 640) % 640 // 128, start % 128)
                    tb = (ta + 1) % TILES
                    if j == 0:
                        ta, tb = (0, 0) if side_of == 0 else (3, 3)
                    for m in range(NM):
                        rows = pl.ds(m, 8, stride=NM)
                        shift = (m - off) % 128
                        cc = (lane - m) & 127
                        y = jnp.where(
                            cc < 128 - off,
                            pltpu.roll(ref[ta, rows, :], shift, axis=1), pltpu.roll(ref[tb, rows, :], shift, axis=1),
                        )
                        if ref is own:
                            sbuf[j, m] = y
                            continue
                        o = sbuf[j, m]
                        y = jnp.where(last, o, y)
                        s_m = 0.25 * (o + y)
                        if j == 0:
                            s_m = jnp.where(cc >= 1 if side_of == 0 else cc < 127, s_m, 0.0)
                        sbuf[j, m] = s_m
                        tbuf[j, m] = o - y

    for first, second in ((own_t, side_ot), (own_h, side_oh), (corner_t, side_t), (corner_h, side_h)):
        when(first[2], first[0].wait_recv)
        when(second[1], second[0].start)
    build(range(4), own)
    when(next_mid[2], next_mid[0].wait_recv)
    when(side_m[1], side_m[0].start)

    lo, hi = (jnp.where(tx == 0, 1, 0), jnp.where(tx == 0, 128, 127))

    def coefficients(j):
        s_list = [sbuf[j, m] for m in range(NM)]
        for frame in range(2):
            left = [pltpu.roll(v, 1 + frame, axis=1) for v in s_list]
            right = s_list if frame else [pltpu.roll(v, 127, axis=1) for v in s_list]
            above = pltpu.roll(pltpu.roll(s_list[NM - 1], 1, axis=0), 113 + frame, axis=1)
            below = pltpu.roll(pltpu.roll(s_list[0], 7, axis=0), 15 + frame, axis=1)
            for m in range(NM):
                gx = right[m] - left[m]
                gy = (right[m + 1] if m < NM - 1 else below) - (left[m - 1] if m else above)
                gt = pltpu.roll(tbuf[j, m], 1, axis=1) if frame else tbuf[j, m]
                mask = tmask[m]
                if j == 0:
                    cc = (lane - (m + frame)) & 127
                    mask = jnp.where((cc >= lo) & (cc < hi), mask, 0.0)
                xx = gx * gx
                yy = ALPHA + gy * gy
                r = mask / (xx + yy)
                q = 0.25 * r
                rt = gt * r
                values = (yy * q, gx * gy * q, gx * rt, (ALPHA + xx) * q, gy * rt)
                for k, value in enumerate(values):
                    coef[frame, k, j, m] = value
                if frame:
                    x[0, j, m] = values[2]
                    x[1, j, m] = values[4]

    build(range(4), nxt)
    for j in range(4):
        coefficients(j)
    for copy, _, receives in (side, side_ot, side_oh):
        when(receives, copy.wait_recv)
    build((4,), own)
    for copy, _, receives in (side_m, side_t, side_h):
        when(receives, copy.wait_recv)
    build((4,), nxt)
    coefficients(4)

    def sweep(kind):
        for j in range(TILES):
            means = []
            for c in range(2):
                f = [x[c, j, m] for m in range(NM)]
                below = pltpu.roll(f[0], 7, axis=0)
                above = pltpu.roll(f[NM - 1], 1, axis=0)
                g = [f[m] + f[m + 1] for m in range(NM - 1)]
                if kind == 0:
                    one = [pltpu.roll(y, 126, axis=1) for y in g]
                    one.append(pltpu.roll(f[NM - 1], 126, axis=1) + pltpu.roll(below, 14, axis=1))
                    two = [pltpu.roll(above, 112, axis=1) + f[0]] + g
                else:
                    one = g + [f[NM - 1] + pltpu.roll(below, 16, axis=1)]
                    two = [pltpu.roll(above, 114, axis=1) + pltpu.roll(f[0], 2, axis=1)]
                    two += [pltpu.roll(y, 2, axis=1) for y in g]
                means.append([one[m] + two[m] for m in range(NM)])
            for m in range(NM):
                mu, mv = (means[0][m], means[1][m])
                k = [coef[kind, i, j, m] for i in range(5)]
                x[0, j, m] = (k[0] * mu - k[1] * mv) + k[2]
                x[1, j, m] = (k[3] * mv - k[1] * mu) + k[4]

    def two_sweeps(_, carry):
        sweep(1)
        sweep(0)
        return carry

    sweep(0)
    for _ in range((SWEEPS - 2) // 2):
        two_sweeps(0, 0)

    for j in range(TILES):
        for c in range(2):
            for p in range(4):
                f = [pltpu.roll(x[c, j, m], (128 - m) & 127, axis=1) if m else x[c, j, m] for m in range(4 * p, 4 * p + 4)]
                pooled[pl.ds(8 * (4 * c + p), 8), pl.ds(128 * j, 128)] = (f[0] + f[1]) + (f[2] + f[3])

    coarse = dot3(pooled[...], pool_w[...])
    crow = 4 * sub + (16 * ty - 8)
    cmask = []
    for p in range(4):
        row_in = (crow + p >= 0) & (crow + p < 16 * n_ty)
        per_tile = []
        for t in range(2):
            q = lane + (128 * tx + (-8 if t == 0 else 104))
            per_tile.append(jnp.where(row_in & (q >= 0) & (q < 256), 1.0, 0.0))
        cmask.append(per_tile)
    e = [
        [[coarse[8 * (4 * c + p) : 8 * (4 * c + p) + 8, 128 * t : 128 * t + 128] for p in range(4)] for t in range(2)]
        for c in range(2)
    ]

    def mesh_sweep(y, t):
        out = []
        for p in range(4):
            up = y[p - 1] if p else pltpu.roll(y[3], 1, axis=0)
            down = y[p + 1] if p < 3 else pltpu.roll(y[0], 7, axis=0)
            total = (up + down) + (pltpu.roll(y[p], 1, axis=1) + pltpu.roll(y[p], 127, axis=1))
            out.append(total * cmask[p][t])
        return out

    def pack(e):
        out = []
        for p in range(4):
            both = [
                jnp.where(lane < 116, pltpu.roll(e[c][0][p], 120, axis=1), pltpu.roll(e[c][1][p], 104, axis=1))
                for c in range(2)
            ]
            out.append(jnp.where(sub < 4, pltpu.roll(both[0], 6, axis=0), pltpu.roll(both[1], 2, axis=0)))
        return out

    terms = [e]

    def weight(d, b):
        value = TABLE[N_SEC - 1, d, b]
        for src in range(N_SEC - 1):
            value = jnp.where(sec == src, TABLE[src, d, b], value)
        return value

    def combine(d):
        total = None
        for b in range(RELAX + 1):
            if not TABLE[:, d, b].any():
                continue
            w = weight(d, b)
            part = [[[w * y for y in terms[b][c][t]] for t in range(2)] for c in range(2)]
            total = part if total is None else [
                [[y + z for y, z in zip(total[c][t], part[c][t])] for t in range(2)] for c in range(2)
            ]
        return pack(total)

    exchanges = []
    for d in (2, 1, 3):
        while any(TABLE[:, d, b].any() for b in range(len(terms), RELAX + 1)):
            e = [[mesh_sweep(e[c][t], t) for t in range(2)] for c in range(2)]
            terms.append(e)
        for p, term in enumerate(combine(d)):
            sent[d - 1, p] = term
        copy = pltpu.make_async_remote_copy(
            src_ref=sent.at[d - 1], dst_ref=got.at[d - 1],
            send_sem=csend_sem.at[d - 1], recv_sem=crecv_sem.at[d - 1],
            device_id=others[d - 1], device_id_type=MESH,
        )
        copy.start()
        exchanges.append(copy)
    while len(terms) <= RELAX:
        e = [[mesh_sweep(e[c][t], t) for t in range(2)] for c in range(2)]
        terms.append(e)
    mine = combine(0)

    for side_of in range(2):
        @pl.when(tx == side_of)
        def _(side_of=side_of):
            for m in range(NM):
                both = [
                    jnp.where(sub < 4, pltpu.roll(x[0, j, m], 6, axis=0), pltpu.roll(x[1, j, m], 2, axis=0))
                    for j in range(TILES)
                ]
                for i in range(4):
                    sh1, sh2 = (127 - 24 * i, 103 - 24 * i) if side_of == 0 else (24 * i + 1, 25 + 24 * i)
                    from_edge = lane if side_of == 0 else 127 - lane
                    packed[i, m] = jnp.where(
                        from_edge < 115 - 24 * i,
                        pltpu.roll(both[i], (sh1 - m) % 128, axis=1), pltpu.roll(both[i + 1], (sh2 - m) % 128, axis=1),
                    )

    for copy, sends, _ in copies:
        when(sends, copy.wait_send)

    for copy in exchanges:
        copy.wait_recv()
    disp = [((mine[p] + got[0, p]) + (got[1, p] + got[2, p])) for p in range(4)]
    back = dot3(jnp.concatenate(disp, axis=0), up_w[...])
    for m in range(NM):
        p = m // 4
        local = NM * (sub & 3) + m
        tissue = ((local + lax.shift_right_logical(k_own, 1)) & (ROWS - 1)) < k_own
        for i in range(4):
            a = jnp.where(tx == 0, i, 3 - i)
            value = packed[i, m] + jnp.where(tissue, back[8 * p : 8 * p + 8, 128 * i : 128 * i + 128], 0.0)
            out_ref[pl.ds((m // 8) * 32 + m % 8 + 8 * a, 8, stride=64), :] = value
    for copy in exchanges:
        copy.wait_send()


def shards(images, tissue_rows):
    vmem = pltpu.VMEM
    flat = pl.pallas_call(
        kernel,
        out_shape=jax.ShapeDtypeStruct((2 * ROWS * 4, 128), F32),
        in_specs=[pl.BlockSpec(memory_space=pltpu.HBM), pl.BlockSpec(memory_space=pltpu.HBM)],
        out_specs=pl.BlockSpec(memory_space=pltpu.VMEM),
        scratch_shapes=[
            vmem((TILES, EXT, 128), F32),
            vmem((TILES, EXT, 128), F32),
            vmem((TILES, NM, 8, 128), F32),
            vmem((TILES, NM, 8, 128), F32),
            vmem((NM, 8, 128), F32),
            vmem((2, 5, TILES, NM, 8, 128), F32),
            vmem((2, TILES, NM, 8, 128), F32),
            vmem((64, TILES * 128), F32),
            vmem((TILES * 128, 256), BF16),
            vmem((128, COLS), BF16),
            vmem((3, 4, 8, 128), F32),
            vmem((3, 4, 8, 128), F32),
            vmem((4, NM, 8, 128), F32),
            pltpu.SMEM((32,), jnp.int32),
            pltpu.SemaphoreType.DMA((5,)),
            pltpu.SemaphoreType.DMA((11,)),
            pltpu.SemaphoreType.DMA((11,)),
            pltpu.SemaphoreType.DMA((3,)),
            pltpu.SemaphoreType.DMA((3,)),
        ],
        compiler_params=pltpu.CompilerParams(
            collective_id=0, has_side_effects=True, vmem_limit_bytes=24 * 1024 * 1024
        ),
        name="align",
    )(*(pltpu.with_memory_space_constraint(y, pltpu.HBM) for y in (tissue_rows, images)))
    tiles = flat.reshape(2, ROWS // 8, 4, 8, 128).transpose(0, 1, 3, 2, 4)
    return tiles.reshape(2, 1, ROWS, COLS)


def solution(mesh):
    return jax.shard_map(
        shards, mesh=mesh, in_specs=(P("sec", "ty", "tx"), P()), out_specs=P(None, "sec", "ty", "tx"), check_vma=False
    )
```

```python
import functools

import jax
import jax.numpy as jnp
import numpy as np
from jax import lax
from jax.experimental import pallas as pl
from jax.experimental.pallas import tpu as pltpu
from jax.sharding import PartitionSpec as P

MESH = pl.DeviceIdType.MESH
F32 = jnp.float32
BF16 = jnp.bfloat16

SWEEPS = 12
RELAX = 4
ALPHA = 0.5
STACK = 1.0
COUPLE = 0.5
TOTAL = 5.0

N_SEC = 4
ROWS = 64
COLS = 512
HALO = 32
REACH = 29
EXT = ROWS + 2 * HALO
NM = EXT // 8
TILES = 5
STEP = 104


def section_table():
    w = {(0, 0): 1.0}
    for _ in range(RELAX):
        new = {(0, 0): 1.0}
        for (a, b), value in w.items():
            new[(a + 1, b)] = new.get((a + 1, b), 0.0) + value
            new[(a, b + 1)] = new.get((a, b + 1), 0.0) + value
        w = {key: value / TOTAL for key, value in new.items()}
    path = np.zeros((N_SEC, N_SEC))
    for i in range(N_SEC - 1):
        path[i, i + 1] = path[i + 1, i] = STACK
    table = np.zeros((N_SEC, N_SEC, RELAX + 1))
    for (a, b), value in w.items():
        power = np.linalg.matrix_power(path, a)
        for src in range(N_SEC):
            for shift in range(N_SEC):
                table[src, shift, b] += value * power[(src + shift) % N_SEC, src] * COUPLE**b
    return table.astype(np.float32)


TABLE = section_table()


def split3(x):
    hi = x.astype(BF16)
    rest = x - hi.astype(F32)
    mid = rest.astype(BF16)
    low = (rest - mid.astype(F32)).astype(BF16)
    return jnp.concatenate([hi, mid, low], axis=0)


def dot3(x, w):
    n = x.shape[0]
    y = jnp.dot(split3(x), w, preferred_element_type=F32)
    return y[:n] + y[n : 2 * n] + y[2 * n :]


def kernel(
    tissue_hbm, img_ref, out_ref,
    own, nxt, sbuf, tbuf, tmask, coef, x, pooled, pool_w, up_w, sent, got, back, tissue_ref,
    load_sem, send_sem, recv_sem, csend_sem, crecv_sem,
):
    n_ty = lax.axis_size("ty")
    sec = lax.axis_index("sec")
    ty = lax.axis_index("ty")
    tx = lax.axis_index("tx")
    has_before, has_after = (ty > 0, ty < n_ty - 1)
    has_next, has_prev = (sec < N_SEC - 1, sec > 0)
    ty_b, ty_a = (jnp.maximum(ty - 1, 0), jnp.minimum(ty + 1, n_ty - 1))
    sec_n, sec_p = (jnp.minimum(sec + 1, N_SEC - 1), jnp.maximum(sec - 1, 0))
    partner = {"tx": 1 - tx}
    others = [{"sec": (sec + d) & (N_SEC - 1)} for d in range(1, N_SEC)]
    top, mid, low = (pl.ds(HALO, HALO), pl.ds(HALO, ROWS), pl.ds(ROWS, HALO))
    head, tail = (pl.ds(0, HALO), pl.ds(HALO + ROWS, HALO))
    four = pl.ds(0, 4)

    for ref in (own, nxt):
        for j in range(4):
            for at in (0, EXT - 8):
                ref[j, pl.ds(at, 8), :] = jnp.zeros((8, 128), F32)

    barrier = pltpu.get_barrier_semaphore()
    meets = []
    for has_sec, s_at in ((has_next, sec_n), (has_prev, sec_p)):
        meets += [
            (has_sec & has_before, {"sec": s_at, "ty": ty_b}),
            (has_sec & has_after, {"sec": s_at, "ty": ty_a}),
        ]
    meets += [(has_before, {"ty": ty_b}), (has_after, {"ty": ty_a})]
    meets += [(None, others[d]) for d in (1, 0, 2)] + [(None, partner)]

    def when(cond, fn):
        if cond is None:
            fn()
        else:
            pl.when(cond)(fn)

    n_meets = 0
    for cond, device in meets:
        when(cond, lambda device=device: pl.semaphore_signal(barrier, inc=1, device_id=device, device_id_type=MESH))
        n_meets = n_meets + (1 if cond is None else cond.astype(jnp.int32))

    loads = [
        pltpu.make_async_copy(img_ref.at[0, :, pl.ds(128 * j, 128)], own.at[j, mid], load_sem.at[j])
        for j in range(4)
    ]
    for load in loads:
        load.start()
    tissue_load = pltpu.make_async_copy(tissue_hbm, tissue_ref, load_sem.at[4])
    tissue_load.start()

    lane = lax.broadcasted_iota(jnp.int32, (8, 128), 1)
    sub = lax.broadcasted_iota(jnp.int32, (8, 128), 0)

    def start_of(j):
        return jnp.where(tx == 0, STEP * j - 1, 385 - STEP * j)

    def clear(rows):
        def body():
            for ref in (own, nxt):
                for j in range(TILES):
                    ref[j, rows, :] = jnp.zeros((HALO, 128), F32)
        return body

    n_id = lax.broadcasted_iota(jnp.int32, (128, 256), 1)
    k_id = lax.broadcasted_iota(jnp.int32, (128, 256), 0)
    q_of = jnp.where(n_id < 128, n_id - 8, n_id - 24)
    for j in range(TILES):
        col = k_id + start_of(j)
        lo, hi = (12, 115)
        if j == 0:
            lo = jnp.where(tx == 0, 1, 12)
            hi = jnp.where(tx == 0, 115, 126)
        hit = (k_id >= lo) & (k_id <= hi) & (lax.shift_right_arithmetic(col, 2) == q_of)
        pool_w[pl.ds(128 * j, 128), :] = jnp.where(hit, 0.0625, 0.0).astype(BF16)
    un = lax.broadcasted_iota(jnp.int32, (128, 128), 1)
    uq = lax.broadcasted_iota(jnp.int32, (128, 128), 0)
    for i in range(4):
        a = jnp.where(tx == 0, i, 3 - i)
        hit = lax.shift_right_arithmetic(un + 128 * a, 2) == uq
        up_w[:, pl.ds(128 * i, 128)] = jnp.where(hit, 1.0, 0.0).astype(BF16)
    pl.when(jnp.logical_not(has_before))(clear(head))
    pl.when(jnp.logical_not(has_after))(clear(tail))

    tissue_load.wait()
    k_own = tissue_ref[ty]
    k_before = jnp.where(has_before, tissue_ref[ty_b], 0)
    k_after = jnp.where(has_after, tissue_ref[ty_a], 0)
    limit = jnp.where(sub < 2, k_before, jnp.where(sub < 6, k_own, k_after))
    half = lax.shift_right_logical(limit, 1)
    for m in range(NM):
        tmask[m] = jnp.where(((NM * sub + (m + HALO) + half) & (ROWS - 1)) < limit, 1.0, 0.0)
    last = jnp.logical_not(has_next)

    for load in loads:
        load.wait()
    pl.semaphore_wait(barrier, n_meets)

    edge = jnp.where(tx == 0, 3, 0)

    def remote(k, src, dst, device):
        return pltpu.make_async_remote_copy(
            src_ref=src, dst_ref=dst, send_sem=send_sem.at[k], recv_sem=recv_sem.at[k],
            device_id=device, device_id_type=MESH,
        )

    up_b, dn_a = (has_before, has_after)
    corner_t = (remote(0, own.at[four, pl.ds(HALO, REACH)], nxt.at[four, pl.ds(HALO + ROWS, REACH)], {"sec": sec_p, "ty": ty_b}), has_prev & up_b, has_next & dn_a)
    corner_h = (remote(1, own.at[four, pl.ds(HALO + ROWS - REACH, REACH)], nxt.at[four, pl.ds(HALO - REACH, REACH)], {"sec": sec_p, "ty": ty_a}), has_prev & dn_a, has_next & up_b)
    next_mid = (remote(2, own.at[four, mid], nxt.at[four, mid], {"sec": sec_p}), has_prev, has_next)
    own_t = (remote(3, own.at[four, pl.ds(HALO, REACH)], own.at[four, pl.ds(HALO + ROWS, REACH)], {"ty": ty_b}), up_b, dn_a)
    own_h = (remote(4, own.at[four, pl.ds(HALO + ROWS - REACH, REACH)], own.at[four, pl.ds(HALO - REACH, REACH)], {"ty": ty_a}), dn_a, up_b)
    side = (remote(5, own.at[edge, mid], own.at[4, mid], partner), None, None)
    side_ot = (remote(6, own.at[edge, tail], own.at[4, tail], partner), dn_a, dn_a)
    side_oh = (remote(7, own.at[edge, head], own.at[4, head], partner), up_b, up_b)
    side_m = (remote(8, nxt.at[edge, mid], nxt.at[4, mid], partner), has_next, has_next)
    side_t = (remote(9, nxt.at[edge, tail], nxt.at[4, tail], partner), has_next & dn_a, has_next & dn_a)
    side_h = (remote(10, nxt.at[edge, head], nxt.at[4, head], partner), has_next & up_b, has_next & up_b)
    copies = [corner_t, corner_h, next_mid, own_t, own_h, side, side_ot, side_oh, side_m, side_t, side_h]

    for copy, sends, _ in copies[:6]:
        when(sends, copy.start)
    def build(tiles, ref):
        for side_of in range(2):
            @pl.when(tx == side_of)
            def _(side_of=side_of):
                for j in tiles:
                    start = STEP * j - 1 if side_of == 0 else 385 - STEP * j
                    ta, off = ((start + 640) % 640 // 128, start % 128)
                    tb = (ta + 1) % TILES
                    if j == 0:
                        ta, tb = (0, 0) if side_of == 0 else (3, 3)
                    for m in range(NM):
                        rows = pl.ds(m, 8, stride=NM)
                        shift = (m - off) % 128
                        cc = (lane - m) & 127
                        y = jnp.where(
                            cc < 128 - off,
                            pltpu.roll(ref[ta, rows, :], shift, axis=1), pltpu.roll(ref[tb, rows, :], shift, axis=1),
                        )
                        if ref is own:
                            sbuf[j, m] = y
                            continue
                        o = sbuf[j, m]
                        y = jnp.where(last, o, y)
                        s_m = 0.25 * (o + y)
                        if j == 0:
                            s_m = jnp.where(cc >= 1 if side_of == 0 else cc < 127, s_m, 0.0)
                        sbuf[j, m] = s_m
                        tbuf[j, m] = o - y

    for first, second in ((own_t, side_ot), (own_h, side_oh), (corner_t, side_t), (corner_h, side_h)):
        when(first[2], first[0].wait_recv)
        when(second[1], second[0].start)
    build(range(4), own)
    when(next_mid[2], next_mid[0].wait_recv)
    when(side_m[1], side_m[0].start)

    lo, hi = (jnp.where(tx == 0, 1, 0), jnp.where(tx == 0, 128, 127))

    def coefficients(j):
        s_list = [sbuf[j, m] for m in range(NM)]
        for frame in range(2):
            left = [pltpu.roll(v, 1 + frame, axis=1) for v in s_list]
            right = s_list if frame else [pltpu.roll(v, 127, axis=1) for v in s_list]
            above = pltpu.roll(pltpu.roll(s_list[NM - 1], 1, axis=0), 113 + frame, axis=1)
            below = pltpu.roll(pltpu.roll(s_list[0], 7, axis=0), 15 + frame, axis=1)
            for m in range(NM):
                gx = right[m] - left[m]
                gy = (right[m + 1] if m < NM - 1 else below) - (left[m - 1] if m else above)
                gt = pltpu.roll(tbuf[j, m], 1, axis=1) if frame else tbuf[j, m]
                mask = tmask[m]
                if j == 0:
                    cc = (lane - (m + frame)) & 127
                    mask = jnp.where((cc >= lo) & (cc < hi), mask, 0.0)
                xx = gx * gx
                yy = ALPHA + gy * gy
                r = mask / (xx + yy)
                q = 0.25 * r
                rt = gt * r
                values = (yy * q, gx * gy * q, gx * rt, (ALPHA + xx) * q, gy * rt)
                for k, value in enumerate(values):
                    coef[frame, k, j, m] = value
                if frame:
                    x[0, j, m] = values[2]
                    x[1, j, m] = values[4]

    build(range(4), nxt)
    for j in range(4):
        coefficients(j)
    for copy, _, receives in (side, side_ot, side_oh):
        when(receives, copy.wait_recv)
    build((4,), own)
    for copy, _, receives in (side_m, side_t, side_h):
        when(receives, copy.wait_recv)
    build((4,), nxt)
    coefficients(4)

    def sweep(kind):
        for j in range(TILES):
            means = []
            for c in range(2):
                f = [x[c, j, m] for m in range(NM)]
                below = pltpu.roll(f[0], 7, axis=0)
                above = pltpu.roll(f[NM - 1], 1, axis=0)
                g = [f[m] + f[m + 1] for m in range(NM - 1)]
                if kind == 0:
                    one = [pltpu.roll(y, 126, axis=1) for y in g]
                    one.append(pltpu.roll(f[NM - 1], 126, axis=1) + pltpu.roll(below, 14, axis=1))
                    two = [pltpu.roll(above, 112, axis=1) + f[0]] + g
                else:
                    one = g + [f[NM - 1] + pltpu.roll(below, 16, axis=1)]
                    two = [pltpu.roll(above, 114, axis=1) + pltpu.roll(f[0], 2, axis=1)]
                    two += [pltpu.roll(y, 2, axis=1) for y in g]
                means.append([one[m] + two[m] for m in range(NM)])
            for m in range(NM):
                mu, mv = (means[0][m], means[1][m])
                k = [coef[kind, i, j, m] for i in range(5)]
                x[0, j, m] = (k[0] * mu - k[1] * mv) + k[2]
                x[1, j, m] = (k[3] * mv - k[1] * mu) + k[4]

    def two_sweeps(_, carry):
        sweep(1)
        sweep(0)
        return carry

    sweep(0)
    for _ in range((SWEEPS - 2) // 2):
        two_sweeps(0, 0)

    for j in range(TILES):
        for c in range(2):
            for p in range(4):
                f = [pltpu.roll(x[c, j, m], (128 - m) & 127, axis=1) if m else x[c, j, m] for m in range(4 * p, 4 * p + 4)]
                pooled[pl.ds(8 * (4 * c + p), 8), pl.ds(128 * j, 128)] = (f[0] + f[1]) + (f[2] + f[3])

    coarse = dot3(pooled[...], pool_w[...])
    crow = 4 * sub + (16 * ty - 8)
    cmask = []
    for p in range(4):
        row_in = (crow + p >= 0) & (crow + p < 16 * n_ty)
        per_tile = []
        for t in range(2):
            q = lane + (128 * tx + (-8 if t == 0 else 104))
            per_tile.append(jnp.where(row_in & (q >= 0) & (q < 256), 1.0, 0.0))
        cmask.append(per_tile)
    e = [
        [[coarse[8 * (4 * c + p) : 8 * (4 * c + p) + 8, 128 * t : 128 * t + 128] for p in range(4)] for t in range(2)]
        for c in range(2)
    ]

    def mesh_sweep(y, t):
        out = []
        for p in range(4):
            up = y[p - 1] if p else pltpu.roll(y[3], 1, axis=0)
            down = y[p + 1] if p < 3 else pltpu.roll(y[0], 7, axis=0)
            total = (up + down) + (pltpu.roll(y[p], 1, axis=1) + pltpu.roll(y[p], 127, axis=1))
            out.append(total * cmask[p][t])
        return out

    def pack(e):
        out = []
        for p in range(4):
            both = [
                jnp.where(lane < 116, pltpu.roll(e[c][0][p], 120, axis=1), pltpu.roll(e[c][1][p], 104, axis=1))
                for c in range(2)
            ]
            out.append(jnp.where(sub < 4, pltpu.roll(both[0], 6, axis=0), pltpu.roll(both[1], 2, axis=0)))
        return out

    terms = [e]

    def weight(d, b):
        value = TABLE[N_SEC - 1, d, b]
        for src in range(N_SEC - 1):
            value = jnp.where(sec == src, TABLE[src, d, b], value)
        return value

    def combine(d):
        total = None
        for b in range(RELAX + 1):
            if not TABLE[:, d, b].any():
                continue
            w = weight(d, b)
            part = [[[w * y for y in terms[b][c][t]] for t in range(2)] for c in range(2)]
            total = part if total is None else [
                [[y + z for y, z in zip(total[c][t], part[c][t])] for t in range(2)] for c in range(2)
            ]
        return pack(total)

    exchanges = []
    for d in (2, 1, 3):
        while any(TABLE[:, d, b].any() for b in range(len(terms), RELAX + 1)):
            e = [[mesh_sweep(e[c][t], t) for t in range(2)] for c in range(2)]
            terms.append(e)
        for p, term in enumerate(combine(d)):
            sent[d - 1, p] = term
        copy = pltpu.make_async_remote_copy(
            src_ref=sent.at[d - 1], dst_ref=got.at[d - 1],
            send_sem=csend_sem.at[d - 1], recv_sem=crecv_sem.at[d - 1],
            device_id=others[d - 1], device_id_type=MESH,
        )
        copy.start()
        exchanges.append(copy)
    while len(terms) <= RELAX:
        e = [[mesh_sweep(e[c][t], t) for t in range(2)] for c in range(2)]
        terms.append(e)
    mine = combine(0)

    for side_of in range(2):
        @pl.when(tx == side_of)
        def _(side_of=side_of):
            for m in range(NM):
                both = [
                    jnp.where(sub < 4, pltpu.roll(x[0, j, m], 6, axis=0), pltpu.roll(x[1, j, m], 2, axis=0))
                    for j in range(TILES)
                ]
                for i in range(4):
                    sh1, sh2 = (127 - 24 * i, 103 - 24 * i) if side_of == 0 else (24 * i + 1, 25 + 24 * i)
                    from_edge = lane if side_of == 0 else 127 - lane
                    a = i if side_of == 0 else 3 - i
                    out_ref[pl.ds((m // 8) * 32 + m % 8 + 8 * a, 8, stride=64), :] = jnp.where(
                        from_edge < 115 - 24 * i,
                        pltpu.roll(both[i], (sh1 - m) % 128, axis=1), pltpu.roll(both[i + 1], (sh2 - m) % 128, axis=1),
                    )

    for copy, sends, _ in copies:
        when(sends, copy.wait_send)

    for copy in exchanges:
        copy.wait_recv()
    disp = [((mine[p] + got[0, p]) + (got[1, p] + got[2, p])) for p in range(4)]
    back[...] = dot3(jnp.concatenate(disp, axis=0), up_w[...])
    for r in range(ROWS // 8):
        tissue = ((8 * r + sub + lax.shift_right_logical(k_own, 1)) & (ROWS - 1)) < k_own
        for c in range(2):
            first = 8 * (2 * r % 4) + 4 * c + r // 2
            for i in range(4):
                at = pl.ds((8 * c + r) * 32 + 8 * jnp.where(tx == 0, i, 3 - i), 8)
                columns = pl.ds(128 * i, 128)
                value = jnp.where(
                    sub < 4,
                    jnp.broadcast_to(back[pl.ds(first, 1), columns], (8, 128)),
                    jnp.broadcast_to(back[pl.ds(first + 8, 1), columns], (8, 128)),
                )
                out_ref[at, :] = out_ref[at, :] + jnp.where(tissue, value, 0.0)
    for copy in exchanges:
        copy.wait_send()


def shards(images, tissue_rows):
    vmem = pltpu.VMEM
    flat = pl.pallas_call(
        kernel,
        out_shape=jax.ShapeDtypeStruct((2 * ROWS * 4, 128), F32),
        in_specs=[pl.BlockSpec(memory_space=pltpu.HBM), pl.BlockSpec(memory_space=pltpu.HBM)],
        out_specs=pl.BlockSpec(memory_space=pltpu.VMEM),
        scratch_shapes=[
            vmem((TILES, EXT, 128), F32),
            vmem((TILES, EXT, 128), F32),
            vmem((TILES, NM, 8, 128), F32),
            vmem((TILES, NM, 8, 128), F32),
            vmem((NM, 8, 128), F32),
            vmem((2, 5, TILES, NM, 8, 128), F32),
            vmem((2, TILES, NM, 8, 128), F32),
            vmem((64, TILES * 128), F32),
            vmem((TILES * 128, 256), BF16),
            vmem((128, COLS), BF16),
            vmem((3, 4, 8, 128), F32),
            vmem((3, 4, 8, 128), F32),
            vmem((32, COLS), F32),
            pltpu.SMEM((32,), jnp.int32),
            pltpu.SemaphoreType.DMA((5,)),
            pltpu.SemaphoreType.DMA((11,)),
            pltpu.SemaphoreType.DMA((11,)),
            pltpu.SemaphoreType.DMA((3,)),
            pltpu.SemaphoreType.DMA((3,)),
        ],
        compiler_params=pltpu.CompilerParams(
            collective_id=0, has_side_effects=True, vmem_limit_bytes=24 * 1024 * 1024
        ),
        name="align",
    )(*(pltpu.with_memory_space_constraint(y, pltpu.HBM) for y in (tissue_rows, images)))
    tiles = flat.reshape(2, ROWS // 8, 4, 8, 128).transpose(0, 1, 3, 2, 4)
    return tiles.reshape(2, 1, ROWS, COLS)


def solution(mesh):
    return jax.shard_map(
        shards, mesh=mesh, in_specs=(P("sec", "ty", "tx"), P()), out_specs=P(None, "sec", "ty", "tx"), check_vma=False
    )
```
